512 devices in a mesh: aux: 128 (over x, z, core), occ: 4 (over y).
Axes of the slice: x: 4, y: 4, z: 16, core: 2. Of those that a mesh axis runs over, the one named last changes fastest.
Arguments:
- half_ints: bfloat16 [8192, 3, 2560], P('aux', None, 'occ'), may hold values from -1.75 to 1.75
- coef_virt: bfloat16 [2048, 2560], P('aux', 'occ'), may hold values from -0.125 to 0.125
- screen: int32 [256, 20], P('aux', 'occ'), may hold values from 0 to 1, as said below
- occ_energy: float32 [512], replicated, may hold values from -2 to -0.3
- virt_energy: float32 [2048], replicated, may hold values from 0.2 to 4
- batch_orbitals: int32 [3], replicated, may hold values from 0 to 511, as said below
Outputs:
- amplitudes: float32 [128, 3, 256, 3, 128], P('aux', None, 'occ')
- gamma: bfloat16 [8192, 3, 2048], P(('aux', 'occ'))
The draws below stay inside these ranges and needn't reach their ends.
Inputs may be any that keep to these rules, and one draw needn't show every extreme that they name: `screen`: 1 where a block of 32 auxiliary and 128 atomic functions is kept, 0 where it is screened out. `batch_orbitals`: 3 distinct occupied orbitals, among them the first and the last.
All inputs are finite; a program needn't handle non-finite values.
Results may differ from the reference program's by a relative error of at most 0.006.
Values may be sent and summed in bfloat16 or wider, within the bound.
No kernel may reach another device: no remote copies, remote signals or barrier semaphores. Data moves between devices by JAX's collectives and lax.ppermute only.
A program may use at most 64 MiB of HBM per device.

```python
import math
import jax
import jax.numpy as jnp
from jax import lax

NOCC = 3
NOCC_ALL = 512
NAO = 2560
NV = 2048
A_BLOCKS = 8
NAUX = 8192
B_BLOCKS = 16
AB = 256
BB = 128
N_AUX = 128


def draw_screen(key, part):
    row_count = NAUX // 32
    col_count = NAO // 128
    level = 30 + 60 * jnp.arange(row_count, dtype=jnp.int32) // max(row_count - 1, 1)
    rolled = jax.random.randint(key, (row_count, col_count), 0, 100)
    return (rolled < level[:, None]).astype(jnp.int32)


def draw_batch_orbitals(key, part):
    first_key, second_key = jax.random.split(jax.random.fold_in(key, 17))
    middle = jax.random.permutation(first_key, NOCC_ALL - 2)[:NOCC - 2].astype(jnp.int32) + 1
    ends = jnp.array([0, NOCC_ALL - 1], dtype=jnp.int32)
    values = jnp.concatenate([ends, middle])
    order = jax.random.permutation(second_key, NOCC)
    return values[order].astype(jnp.int32)


def block_scale(rng, extent, pieces, least, largest):
    def one(axis_at, shards_of):
        steps = jax.random.uniform(jax.random.fold_in(jax.random.fold_in(rng, 6), axis_at), (shards_of,), jnp.float32, least / len(pieces), largest / len(pieces))
        return jnp.repeat(jnp.exp(steps), extent[axis_at] // shards_of).reshape((-1,) + (1,) * (len(extent) - axis_at - 1))

    gain = one(*pieces[0])
    for cut in pieces[1:]:
        gain = gain * one(*cut)
    return gain


def normal_values(key, dims, width, bound, pieces=(), kind=jnp.bfloat16):
    factor_of = block_scale(key, dims, pieces, -0.22, 0.18) if pieces else 1.0
    values = jax.random.normal(key, dims, jnp.float32) * width * factor_of
    return jnp.minimum(jnp.maximum(values, -bound), bound).astype(kind)


def setup_inputs(seed: int = 0) -> dict:
    streams_of = jax.random.split(jax.random.key(seed), 7)
    half_ints = normal_values(streams_of[0], (NAUX, NOCC, NAO), 0.12, 1.75, ((0, 128), (2, 4)))
    coef_virt = normal_values(streams_of[1], (NV, NAO), NAO ** -0.5, 0.125, ((0, 128), (1, 4)))
    screen = draw_screen(jax.random.fold_in(streams_of[6], 71), 0)
    occ_energy = jnp.clip(jax.random.uniform(streams_of[3], (NOCC_ALL,), jnp.float32, -2.0, -0.3), -2.0, -0.3)
    virt_energy = jnp.clip(jnp.exp(jax.random.uniform(streams_of[4], (NV,), jnp.float32, math.log(0.2), math.log(4.0))), 0.2, 4.0)
    batch_orbitals = draw_batch_orbitals(jax.random.fold_in(streams_of[6], 71), 0)
    return {"half_ints": half_ints, "coef_virt": coef_virt, "screen": screen, "occ_energy": occ_energy, "virt_energy": virt_energy, "batch_orbitals": batch_orbitals}


def reference(half_ints, coef_virt, screen, occ_energy, virt_energy, batch_orbitals):
    expanded = jnp.repeat(jnp.repeat(screen, 32, axis=0), 128, axis=1).astype(jnp.bfloat16)
    masked = half_ints * expanded[:, None, :]
    flattened = masked.reshape(NAUX * NOCC, NAO)
    three_index = jnp.dot(flattened, coef_virt.T, preferred_element_type=jnp.float32).astype(jnp.bfloat16)
    three_index = three_index.reshape(NAUX, NOCC, NV)
    slot_energy = occ_energy[batch_orbitals]
    values = three_index.astype(jnp.float32)
    gram_whole = jnp.einsum('pia,pjb->iajb', values, values)
    denominator = (slot_energy[:, None, None, None] + slot_energy[None, None, :, None]
                   - virt_energy[None, :, None, None] - virt_energy[None, None, None, :])
    amps_full = gram_whole / denominator
    mixed_block = (2.0 * amps_full - jnp.transpose(amps_full, (2, 1, 0, 3))).astype(jnp.bfloat16)
    mixed_values = mixed_block.astype(jnp.float32)

    def add_block(block_index, running):
        col_start = (block_index * BB).astype(jnp.int32)
        mix_part = lax.dynamic_slice_in_dim(mixed_values, col_start, BB, 3)
        val_part = lax.dynamic_slice_in_dim(values, col_start, BB, 2)
        partial_value = jnp.einsum('iajb,pjb->pia', mix_part, val_part).astype(jnp.bfloat16)
        partial_value = lax.optimization_barrier(partial_value)
        return running + partial_value.astype(jnp.float32)

    gamma_sum = lax.fori_loop(0, B_BLOCKS, add_block, jnp.zeros((NAUX, NOCC, NV), jnp.float32))
    gamma_rows = gamma_sum.astype(jnp.bfloat16)
    amplitudes = amps_full.reshape(NOCC, A_BLOCKS, AB, NOCC, B_BLOCKS, BB)
    amplitudes = amplitudes.transpose(1, 4, 0, 2, 3, 5).reshape(N_AUX, NOCC, AB, NOCC, BB)
    return amplitudes, gamma_rows
```

```python
import jax
import jax.numpy as jnp
from jax import lax
from jax.sharding import Mesh
from jax.sharding import PartitionSpec as P

BF = jnp.bfloat16
F32 = jnp.float32


def swap_cores(value):
    return lax.ppermute(value, "c", [(0, 1), (1, 0)])


def local(half_ints, coef_virt, screen, occ_energy, virt_energy, batch_orbitals):
    p_rows, nocc, ao_part = half_ints.shape
    nv = virt_energy.shape[0]
    nx, nz, ny = lax.axis_size("x"), lax.axis_size("z"), lax.axis_size("y")
    nl = nz // 2
    x, z, c, y = (lax.axis_index(name) for name in ("x", "z", "c", "y"))
    zh, zl = z // nl, z % nl
    r = p_rows // ny
    wide = nv // nx
    narrow = nv // nz
    half = wide // 2
    share = half // ny

    labels = jnp.arange(occ_energy.shape[0], dtype=jnp.int32)
    onehot = (batch_orbitals[:, None] == labels[None, :]).astype(F32)
    slot_energy = jnp.sum(onehot * occ_energy[None, :], axis=1)

    with jax.named_scope("transform"):
        expanded = jnp.repeat(jnp.repeat(screen, 32, axis=0), 128, axis=1).astype(BF)
        masked = half_ints * expanded[:, None, :]
        masked = masked.reshape(ny, r, nocc, ao_part).transpose(0, 2, 1, 3)
        masked = lax.all_gather(masked, "x", axis=0)
        coef = lax.all_gather(coef_virt, ("z", "c"), axis=0, tiled=True)
        part = jnp.einsum("xyirm,am->yxira", masked, coef, preferred_element_type=F32)
        part = lax.all_to_all(part.astype(BF), "y", split_axis=0, concat_axis=0, tiled=True)
        three = jnp.sum(part.astype(F32), axis=0).astype(BF)
        three = three.transpose(0, 2, 1, 3)

    with jax.named_scope("panels"):
        row = lax.all_gather(three.reshape(nx, r, nocc * wide), "z", axis=0)
        row = row.reshape(nz * nx * r, nocc * wide)
        col = lax.all_to_all(three, "x", split_axis=0, concat_axis=0, tiled=True)
        col = col.reshape(nx, r, nocc, wide // narrow, narrow).transpose(0, 3, 1, 2, 4)
        col = col.reshape(nl, 2, r, nocc * narrow).transpose(1, 0, 2, 3)
        col = col.reshape(nz, r, nocc * narrow)
        col = lax.all_to_all(col, "z", split_axis=0, concat_axis=0, tiled=True)
        col = lax.all_gather(col, "x", axis=0)
        col = col.transpose(1, 0, 2, 3).reshape(nz * nx * r, nocc * narrow)

    with jax.named_scope("gram"):
        gram = lax.dot_general(
            row, col, (((0,), (0,)), ((), ())), preferred_element_type=F32
        )
        gram = gram.reshape(nocc, 2, half, nocc * narrow)
        mine = lax.dynamic_index_in_dim(gram, c, 1, keepdims=False)
        other = lax.dynamic_index_in_dim(gram, 1 - c, 1, keepdims=False)
        gram = mine + swap_cores(other)
        gram = gram.reshape(nocc, ny, share, nocc * narrow).transpose(1, 0, 2, 3)
        gram = lax.all_to_all(gram.astype(BF), "y", split_axis=0, concat_axis=0, tiled=True)
        gram = jnp.sum(gram.astype(F32), axis=0).reshape(nocc, share, nocc, narrow)

    with jax.named_scope("amplitudes"):
        row_energy = lax.dynamic_slice_in_dim(virt_energy, x * wide + c * half + y * share, share, 0)
        col_energy = lax.dynamic_slice_in_dim(virt_energy, (zl * 2 + zh) * narrow, narrow, 0)
        denominators = (
            slot_energy[:, None, None, None]
            + slot_energy[None, None, :, None]
            - row_energy[None, :, None, None]
            - col_energy[None, None, None, :]
        )
        amps = gram / denominators
        mixed = (2.0 * amps - jnp.transpose(amps, (2, 1, 0, 3))).astype(BF)
        swap = []
        for h in range(2):
            for l in range(nl):
                for k in range(2):
                    swap.append(((h * nl + l) * 2 + k, (k * nl + l) * 2 + h))
        own = lax.ppermute(amps, ("z", "c"), swap)
        mixed = lax.all_gather(mixed.reshape(nocc, share, nocc * narrow), "y", axis=1)
        mixed = mixed.reshape(nocc, half, nocc * narrow)
        theirs = swap_cores(mixed)
        low = jnp.where(c == 0, mixed, theirs)
        high = jnp.where(c == 0, theirs, mixed)
        mixed = jnp.concatenate([low[:, None], high[:, None]], axis=1)
        mixed = mixed.reshape(nocc * wide, nocc * narrow)

    with jax.named_scope("gamma"):
        value = jnp.dot(row, mixed, preferred_element_type=F32).astype(BF)
        value = value.reshape(nz, nx, r, nocc * narrow).transpose(1, 0, 2, 3)
        value = lax.all_to_all(value, "x", split_axis=0, concat_axis=0, tiled=True)
        value = jnp.sum(value.astype(F32), axis=0).astype(BF)
        value = lax.all_to_all(value, "z", split_axis=0, concat_axis=0, tiled=True)
        value = value.reshape(2, nl, r, nocc, narrow).transpose(2, 3, 1, 0, 4)
        gamma = value.reshape(r, nocc, nv)
    return own[None], gamma


def solution(mesh):
    fine = Mesh(mesh.devices.reshape(4, mesh.shape["aux"] // 8, 2, mesh.shape["occ"]), ("x", "z", "c", "y"))
    aux = ("x", "z", "c")
    in_specs = (P(aux, None, "y"), P(aux, "y"), P(aux, "y"), P(), P(), P())
    out_specs = (P(aux, None, "y", None, None), P(aux + ("y",), None, None))
    return jax.shard_map(local, mesh=fine, in_specs=in_specs, out_specs=out_specs, check_vma=False)
```

```python
import jax
import jax.numpy as jnp
from jax import lax
from jax.sharding import Mesh
from jax.sharding import PartitionSpec as P

BF = jnp.bfloat16
F32 = jnp.float32


def swap_cores(value):
    return lax.ppermute(value, "c", [(0, 1), (1, 0)])


def exchange(value, axis):
    members, rows, lanes = value.shape
    value = value.reshape(members * rows, lanes)
    value = lax.all_to_all(value, axis, split_axis=0, concat_axis=0, tiled=True)
    return value.reshape(members, rows, lanes)


def by_core(mine, theirs, core):
    return jnp.where(core == 0, mine, theirs), jnp.where(core == 0, theirs, mine)


def local(half_ints, coef_virt, screen, occ_energy, virt_energy, batch_orbitals):
    p_rows, nocc, ao_part = half_ints.shape
    nv = virt_energy.shape[0]
    nx, nz, ny = lax.axis_size("x"), lax.axis_size("z"), lax.axis_size("y")
    nl = nz // 2
    x, z, c, y = (lax.axis_index(name) for name in ("x", "z", "c", "y"))
    zh, zl = z // nl, z % nl
    r = p_rows // ny
    wide = nv // nx
    narrow = nv // nz
    half = wide // 2
    share = half // ny
    ways = wide // narrow

    labels = jnp.arange(occ_energy.shape[0], dtype=jnp.int32)
    onehot = (batch_orbitals[:, None] == labels[None, :]).astype(F32)
    slot_energy = jnp.sum(onehot * occ_energy[None, :], axis=1)

    with jax.named_scope("transform"):
        copies = jnp.broadcast_to(coef_virt[None], (nz,) + coef_virt.shape)
        coef = exchange(copies, "z")
        expanded = jnp.repeat(jnp.repeat(screen, 32, axis=0), 128, axis=1).astype(BF)
        masked = half_ints * expanded[:, None, :]
        masked = masked.reshape(ny, r, nocc, ao_part).transpose(0, 2, 1, 3)
        masked = lax.all_gather(masked.reshape(-1, ao_part), "x", axis=0)
        masked = masked.reshape(nx, ny, nocc, r, ao_part)
        masked, coef = lax.optimization_barrier((masked, coef))
        low, high = by_core(coef, swap_cores(coef), c)
        coef = jnp.stack([low, high], axis=1).reshape(wide, ao_part)
        part = jnp.einsum("xyirm,am->yxira", masked, coef, preferred_element_type=F32)
        part = exchange(part.astype(BF).reshape(ny, nx * nocc * r, wide), "y")
        three = jnp.sum(part.astype(F32), axis=0).astype(BF).reshape(nx, nocc, r, wide)

    with jax.named_scope("panels"):
        row = jnp.concatenate([three[:, i] for i in range(nocc)], axis=-1)
        row = lax.all_gather(row.reshape(nx * r, nocc * wide), "z", axis=0, tiled=True)
        col = exchange(three.reshape(nx, nocc * r, wide), "x")
        col = col.reshape(nx, nocc, r, ways // 2, 2, narrow)
        col = jnp.concatenate(
            [col[:, i].transpose(3, 0, 2, 1, 4).reshape(nz, r, narrow) for i in range(nocc)], axis=-1
        )
        col = exchange(col, "z")
        col = lax.all_gather(col.reshape(nz * r, nocc * narrow), "x", axis=0)
        col = col.reshape(nx, nz, r, nocc * narrow)
        col = col.transpose(1, 0, 2, 3).reshape(nz * nx * r, nocc * narrow)

    with jax.named_scope("gram"):
        gram = lax.dot_general(
            row, col, (((0,), (0,)), ((), ())), preferred_element_type=F32
        )
        gram = gram.reshape(nocc, 2, half, nocc * narrow)
        mine = lax.dynamic_index_in_dim(gram, c, 1, keepdims=False)
        other = lax.dynamic_index_in_dim(gram, 1 - c, 1, keepdims=False)
        gram = mine + swap_cores(other)
        gram = gram.reshape(nocc, ny, share, nocc * narrow).transpose(1, 0, 2, 3)
        gram = exchange(gram.astype(BF).reshape(ny, nocc * share, nocc * narrow), "y")
        gram = jnp.sum(gram.astype(F32), axis=0).reshape(nocc, share, nocc, narrow)

    with jax.named_scope("amplitudes"):
        row_energy = lax.dynamic_slice_in_dim(virt_energy, x * wide + c * half + y * share, share, 0)
        col_energy = lax.dynamic_slice_in_dim(virt_energy, (zl * 2 + zh) * narrow, narrow, 0)
        denominators = (
            slot_energy[:, None, None, None]
            + slot_energy[None, None, :, None]
            - row_energy[None, :, None, None]
            - col_energy[None, None, None, :]
        )
        amps = gram / denominators
        mixed = (2.0 * amps - jnp.transpose(amps, (2, 1, 0, 3))).astype(BF)
        swap = []
        for h in range(2):
            for l in range(nl):
                for k in range(2):
                    swap.append(((h * nl + l) * 2 + k, (k * nl + l) * 2 + h))
        own = lax.ppermute(amps, ("z", "c"), swap)
        mixed = jnp.concatenate([mixed[:, :, j] for j in range(nocc)], axis=-1)
        mixed = lax.all_gather(mixed.reshape(nocc * share, nocc * narrow), "y", axis=0)
        mixed = mixed.reshape(ny, nocc, share, nocc * narrow).transpose(1, 0, 2, 3)
        mixed = mixed.reshape(nocc, half, nocc * narrow)
        low, high = by_core(mixed, swap_cores(mixed), c)
        mixed = jnp.stack([low, high], axis=1).reshape(nocc * wide, nocc * narrow)

    with jax.named_scope("gamma"):
        value = jnp.dot(row, mixed, preferred_element_type=F32).astype(BF)
        value = value.reshape(nz, nx, r, nocc * narrow).transpose(1, 0, 2, 3)
        value = exchange(value.reshape(nx, nz * r, nocc * narrow), "x")
        value = jnp.sum(value.astype(F32), axis=0).astype(BF)
        value = exchange(value.reshape(nz, r, nocc * narrow), "z")
        value = value.reshape(2, nl, r, nocc, narrow).transpose(2, 3, 1, 0, 4)
        gamma = value.reshape(r, nocc, nv)
    return own[None], gamma


def solution(mesh):
    fine = Mesh(mesh.devices.reshape(4, mesh.shape["aux"] // 8, 2, mesh.shape["occ"]), ("x", "z", "c", "y"))
    aux = ("x", "z", "c")
    in_specs = (P(aux, None, "y"), P(aux, "y"), P(aux, "y"), P(), P(), P())
    out_specs = (P(aux, None, "y", None, None), P(aux + ("y",), None, None))
    return jax.shard_map(local, mesh=fine, in_specs=in_specs, out_specs=out_specs, check_vma=False)
```

```python
import jax
import jax.numpy as jnp
from jax import lax
from jax.experimental import pallas as pl
from jax.experimental.pallas import tpu as pltpu
from jax.sharding import Mesh
from jax.sharding import PartitionSpec as P

BF = jnp.bfloat16
F32 = jnp.float32


def swap_cores(value):
    return lax.ppermute(value, "c", [(0, 1), (1, 0)])


def exchange(value, axis):
    members, rows, lanes = value.shape
    value = value.reshape(members * rows, lanes)
    value = lax.all_to_all(value, axis, split_axis=0, concat_axis=0, tiled=True)
    return value.reshape(members, rows, lanes)


def by_core(mine, theirs, core):
    return jnp.where(core == 0, mine, theirs), jnp.where(core == 0, theirs, mine)


def gram_half(row, col, which, nocc, ny):
    k_rows, lanes = row.shape
    half = lanes // nocc // 2
    share = half // ny
    width = col.shape[1]

    def body(which_ref, row_ref, col_ref, out_ref):
        tile = lax.dot_general(
            row_ref[...], col_ref[...], (((0,), (0,)), ((), ())), preferred_element_type=F32
        )
        out_ref[...] = tile.reshape(ny, 1, share, width)

    return pl.pallas_call(
        body,
        out_shape=jax.ShapeDtypeStruct((ny, nocc, share, width), F32),
        grid_spec=pltpu.PrefetchScalarGridSpec(
            num_scalar_prefetch=1,
            grid=(nocc,),
            in_specs=[
                pl.BlockSpec((k_rows, half), lambda i, w: (0, 2 * i + w[0])),
                pl.BlockSpec((k_rows, width), lambda i, w: (0, 0)),
            ],
            out_specs=pl.BlockSpec((ny, 1, share, width), lambda i, w: (0, i, 0, 0)),
        ),
        compiler_params=pltpu.CompilerParams(vmem_limit_bytes=12 * 1024 * 1024),
        cost_estimate=pl.CostEstimate(
            flops=2 * k_rows * nocc * half * width,
            bytes_accessed=2 * k_rows * (nocc * half + width) + 4 * nocc * half * width,
            transcendentals=0,
        ),
        name="gram_half",
    )(which.reshape(1), row, col)


def contract(row, mine, theirs, core, nx, nz):
    k_rows, lanes = row.shape
    ny, nocc, share, width = mine.shape
    half = ny * share
    r = k_rows // nx // nz
    steps = 4
    zs = nz // steps

    def body(core_ref, row_ref, mine_ref, theirs_ref, out_ref, tile_ref):
        @pl.when(pl.program_id(0) == 0)
        def _():
            for i in range(nocc):
                for q in range(ny):
                    for k, ref in enumerate((mine_ref, theirs_ref)):
                        side = core_ref[0] if k == 0 else 1 - core_ref[0]
                        start = (2 * i + side) * half + q * share
                        tile_ref[pl.ds(pl.multiple_of(start, share), share), :] = ref[q, i]

        value = jnp.dot(row_ref[...], tile_ref[...], preferred_element_type=F32).astype(BF)
        value = value.reshape(zs, nx, r, width)
        for k in range(nx):
            out_ref[k] = value[:, k]

    return pl.pallas_call(
        body,
        out_shape=jax.ShapeDtypeStruct((nx, nz, r, width), BF),
        grid_spec=pltpu.PrefetchScalarGridSpec(
            num_scalar_prefetch=1,
            grid=(steps,),
            in_specs=[
                pl.BlockSpec((k_rows // steps, lanes), lambda s, w: (s, 0)),
                pl.BlockSpec((ny, nocc, share, width), lambda s, w: (0, 0, 0, 0)),
                pl.BlockSpec((ny, nocc, share, width), lambda s, w: (0, 0, 0, 0)),
            ],
            out_specs=pl.BlockSpec((nx, zs, r, width), lambda s, w: (0, s, 0, 0)),
            scratch_shapes=[pltpu.VMEM((lanes, width), BF)],
        ),
        compiler_params=pltpu.CompilerParams(vmem_limit_bytes=12 * 1024 * 1024),
        cost_estimate=pl.CostEstimate(
            flops=2 * k_rows * lanes * width,
            bytes_accessed=2 * k_rows * (lanes + width) + 2 * lanes * width,
            transcendentals=0,
        ),
        name="contract",
    )(core.reshape(1), row, mine, theirs)


def amplitudes_of(parts, slot, row_energy, col_energy):
    nocc = slot.shape[0]
    share, narrow = row_energy.shape[0], col_energy.shape[1]
    ways = parts.shape[0]

    def body(slot_ref, row_ref, col_ref, parts_ref, upper_ref, lower_ref, mixed_ref):
        amps = {}
        for i in range(nocc):
            for j in range(nocc):
                at = (pl.ds(i * share, share), pl.ds(j * narrow, narrow))
                total = parts_ref[(0,) + at].astype(F32)
                for k in range(1, ways):
                    total = total + parts_ref[(k,) + at].astype(F32)
                gap = slot_ref[i] + slot_ref[j] - row_ref[...] - col_ref[...]
                amps[i, j] = total / gap
                upper_ref[i, j] = amps[i, j][: share // 2]
                lower_ref[i, j] = amps[i, j][share // 2 :]
        for i in range(nocc):
            for j in range(nocc):
                value = 2.0 * amps[i, j] - amps[j, i]
                mixed_ref[i, :, pl.ds(j * narrow, narrow)] = value.astype(BF)

    vmem = pl.BlockSpec(memory_space=pltpu.VMEM)
    return pl.pallas_call(
        body,
        out_shape=(
            jax.ShapeDtypeStruct((nocc, nocc, share // 2, narrow), F32),
            jax.ShapeDtypeStruct((nocc, nocc, share // 2, narrow), F32),
            jax.ShapeDtypeStruct((nocc, share, nocc * narrow), BF),
        ),
        in_specs=[pl.BlockSpec(memory_space=pltpu.SMEM), vmem, vmem, vmem],
        out_specs=(vmem, vmem, vmem),
        compiler_params=pltpu.CompilerParams(vmem_limit_bytes=12 * 1024 * 1024),
        name="amplitudes_of",
    )(slot, row_energy, col_energy, parts)


def local(half_ints, coef_virt, screen, occ_energy, virt_energy, batch_orbitals):
    p_rows, nocc, ao_part = half_ints.shape
    nv = virt_energy.shape[0]
    nx, nz, ny = lax.axis_size("x"), lax.axis_size("z"), lax.axis_size("y")
    nl = nz // 2
    x, z, c, y = (lax.axis_index(name) for name in ("x", "z", "c", "y"))
    zh, zl = z // nl, z % nl
    r = p_rows // ny
    wide = nv // nx
    narrow = nv // nz
    half = wide // 2
    share = half // ny
    ways = wide // narrow

    labels = jnp.arange(occ_energy.shape[0], dtype=jnp.int32)
    onehot = (batch_orbitals[:, None] == labels[None, :]).astype(F32)
    slot_energy = jnp.sum(onehot * occ_energy[None, :], axis=1)

    with jax.named_scope("transform"):
        copies = jnp.broadcast_to(coef_virt[None], (nz,) + coef_virt.shape)
        coef = exchange(copies, "z")
        expanded = jnp.repeat(jnp.repeat(screen, 32, axis=0), 128, axis=1).astype(BF)
        masked = half_ints * expanded[:, None, :]
        masked = masked.reshape(ny, r, nocc, ao_part).transpose(0, 2, 1, 3)
        masked = lax.all_gather(masked.reshape(-1, ao_part), "x", axis=0)
        masked = masked.reshape(nx, ny, nocc, r, ao_part)
        masked, coef = lax.optimization_barrier((masked, coef))
        low, high = by_core(coef, swap_cores(coef), c)
        coef = jnp.stack([low, high], axis=1).reshape(wide, ao_part)
        part = jnp.einsum("xyirm,am->yxira", masked, coef, preferred_element_type=F32)
        part = exchange(part.astype(BF).reshape(ny, nx * nocc * r, wide), "y")
        three = jnp.sum(part.astype(F32), axis=0).astype(BF).reshape(nx, nocc, r, wide)

    with jax.named_scope("panels"):
        row = jnp.concatenate([three[:, i] for i in range(nocc)], axis=-1)
        row = lax.all_gather(row.reshape(nx * r, nocc * wide), "z", axis=0, tiled=True)
        col = exchange(three.reshape(nx, nocc * r, wide), "x")
        col = col.reshape(nx, nocc, r, ways // 2, 2, narrow)
        col = jnp.concatenate(
            [col[:, i].transpose(3, 0, 2, 1, 4).reshape(nz, r, narrow) for i in range(nocc)], axis=-1
        )
        col = exchange(col, "z")
        col = lax.all_gather(col.reshape(nz * r, nocc * narrow), "x", axis=0)
        col = col.reshape(nx, nz, r, nocc * narrow)
        col = col.transpose(1, 0, 2, 3).reshape(nz * nx * r, nocc * narrow)

    with jax.named_scope("gram"):
        other = swap_cores(gram_half(row, col, 1 - c, nocc, ny))
        gram = gram_half(row, col, c, nocc, ny) + other
        gram = exchange(gram.astype(BF).reshape(ny, nocc * share, nocc * narrow), "y")

    with jax.named_scope("amplitudes"):
        row_energy = lax.dynamic_slice_in_dim(virt_energy, x * wide + c * half + y * share, share, 0)
        col_energy = lax.dynamic_slice_in_dim(virt_energy, (zl * 2 + zh) * narrow, narrow, 0)
        upper, lower, mixed = amplitudes_of(gram, slot_energy, row_energy[:, None], col_energy[None, :])
        swap = []
        for h in range(2):
            for l in range(nl):
                for k in range(2):
                    swap.append(((h * nl + l) * 2 + k, (k * nl + l) * 2 + h))
        upper = lax.ppermute(upper, ("z", "c"), swap)
        lower = lax.ppermute(lower, ("z", "c"), swap)
        mixed = lax.all_gather(mixed.reshape(nocc * share, nocc * narrow), "y", axis=0)
        mixed, upper = lax.optimization_barrier((mixed, upper))
        mixed = mixed.reshape(ny, nocc, share, nocc * narrow)
        theirs = swap_cores(mixed)

    with jax.named_scope("gamma"):
        value = contract(row, mixed, theirs, c, nx, nz)
        value = exchange(value.reshape(nx, nz * r, nocc * narrow), "x")
        value = jnp.sum(value.astype(F32), axis=0).astype(BF)
        value, lower = lax.optimization_barrier((value, lower))
        value = exchange(value.reshape(nz, r, nocc * narrow), "z")
        value = value.reshape(2, nl, r, nocc, narrow).transpose(2, 3, 1, 0, 4)
        gamma = value.reshape(r, nocc, nv)
    own = jnp.concatenate([upper, lower], axis=2)
    return own.transpose(0, 2, 1, 3)[None], gamma


def solution(mesh):
    fine = Mesh(mesh.devices.reshape(4, mesh.shape["aux"] // 8, 2, mesh.shape["occ"]), ("x", "z", "c", "y"))
    aux = ("x", "z", "c")
    in_specs = (P(aux, None, "y"), P(aux, "y"), P(aux, "y"), P(), P(), P())
    out_specs = (P(aux, None, "y", None, None), P(aux + ("y",), None, None))
    return jax.shard_map(local, mesh=fine, in_specs=in_specs, out_specs=out_specs, check_vma=False)
```

```python
import jax
import jax.numpy as jnp
from jax import lax
from jax.experimental import pallas as pl
from jax.experimental.pallas import tpu as pltpu
from jax.sharding import Mesh
from jax.sharding import PartitionSpec as P

BF = jnp.bfloat16
F32 = jnp.float32
ROOM = 63 * 1024 * 1024


def swap_cores(value):
    return lax.ppermute(value, "c", [(0, 1), (1, 0)])


def exchange(value, axis):
    members, rows, lanes = value.shape
    value = value.reshape(members * rows, lanes)
    value = lax.all_to_all(value, axis, split_axis=0, concat_axis=0, tiled=True)
    return value.reshape(members, rows, lanes)


def by_core(mine, theirs, core):
    return jnp.where(core == 0, mine, theirs), jnp.where(core == 0, theirs, mine)


def gram_half(row, col, which, nocc, ny):
    k_rows, lanes = row.shape
    half = lanes // nocc // 2
    share = half // ny
    width = col.shape[1]

    def body(which_ref, row_ref, col_ref, out_ref, tiles_ref, sems):
        def fetch(i):
            start = pl.multiple_of((2 * i + which_ref[0]) * half, half)
            return pltpu.make_async_copy(row_ref.at[:, pl.ds(start, half)], tiles_ref.at[i], sems.at[i])

        for i in range(nocc):
            fetch(i).start()
        for i in range(nocc):
            fetch(i).wait()
            tile = lax.dot_general(
                tiles_ref[i], col_ref[...], (((0,), (0,)), ((), ())), preferred_element_type=F32
            )
            out_ref[:, i] = tile.reshape(ny, share, width)

    vmem = pl.BlockSpec(memory_space=pltpu.VMEM)
    return pl.pallas_call(
        body,
        out_shape=jax.ShapeDtypeStruct((ny, nocc, share, width), F32),
        in_specs=[pl.BlockSpec(memory_space=pltpu.SMEM), pl.BlockSpec(memory_space=pltpu.HBM), vmem],
        out_specs=vmem,
        scratch_shapes=[pltpu.VMEM((nocc, k_rows, half), BF), pltpu.SemaphoreType.DMA((nocc,))],
        compiler_params=pltpu.CompilerParams(vmem_limit_bytes=ROOM),
        cost_estimate=pl.CostEstimate(
            flops=2 * k_rows * nocc * half * width,
            bytes_accessed=2 * k_rows * (nocc * half + width) + 4 * nocc * half * width,
            transcendentals=0,
        ),
        name="gram_half",
    )(which.reshape(1), row, col)


def contract(row, mine, theirs, core, nx, nz):
    k_rows, lanes = row.shape
    ny, nocc, share, width = mine.shape
    half = ny * share
    r = k_rows // nx // nz
    steps = 4
    zs = nz // steps

    def body(core_ref, row_ref, mine_ref, theirs_ref, out_ref, rows_ref, tile_ref, sems):
        def fetch(s):
            size = k_rows // steps
            return pltpu.make_async_copy(row_ref.at[pl.ds(s * size, size), :], rows_ref.at[s], sems.at[s])

        for s in range(steps):
            fetch(s).start()
        for i in range(nocc):
            for q in range(ny):
                for k, ref in enumerate((mine_ref, theirs_ref)):
                    side = core_ref[0] if k == 0 else 1 - core_ref[0]
                    start = (2 * i + side) * half + q * share
                    tile_ref[pl.ds(pl.multiple_of(start, share), share), :] = ref[q, i]
        for s in range(steps):
            fetch(s).wait()
            value = jnp.dot(rows_ref[s], tile_ref[...], preferred_element_type=F32).astype(BF)
            value = value.reshape(zs, nx, r, width)
            for k in range(nx):
                out_ref[k, s * zs : (s + 1) * zs] = value[:, k]

    vmem = pl.BlockSpec(memory_space=pltpu.VMEM)
    return pl.pallas_call(
        body,
        out_shape=jax.ShapeDtypeStruct((nx, nz, r, width), BF),
        in_specs=[pl.BlockSpec(memory_space=pltpu.SMEM), pl.BlockSpec(memory_space=pltpu.HBM), vmem, vmem],
        out_specs=vmem,
        scratch_shapes=[
            pltpu.VMEM((steps, k_rows // steps, lanes), BF),
            pltpu.VMEM((lanes, width), BF),
            pltpu.SemaphoreType.DMA((steps,)),
        ],
        compiler_params=pltpu.CompilerParams(vmem_limit_bytes=ROOM),
        cost_estimate=pl.CostEstimate(
            flops=2 * k_rows * lanes * width,
            bytes_accessed=2 * k_rows * (lanes + width) + 2 * lanes * width,
            transcendentals=0,
        ),
        name="contract",
    )(core.reshape(1), row, mine, theirs)


def amplitudes_of(parts, slot, row_energy, col_energy):
    nocc = slot.shape[0]
    share, narrow = row_energy.shape[0], col_energy.shape[1]
    ways = parts.shape[0]

    def body(slot_ref, row_ref, col_ref, parts_ref, upper_ref, lower_ref, mixed_ref):
        amps = {}
        for i in range(nocc):
            for j in range(nocc):
                at = (pl.ds(i * share, share), pl.ds(j * narrow, narrow))
                total = parts_ref[(0,) + at].astype(F32)
                for k in range(1, ways):
                    total = total + parts_ref[(k,) + at].astype(F32)
                gap = slot_ref[i] + slot_ref[j] - row_ref[...] - col_ref[...]
                amps[i, j] = total / gap
                upper_ref[i, j] = amps[i, j][: share // 2]
                lower_ref[i, j] = amps[i, j][share // 2 :]
        for i in range(nocc):
            for j in range(nocc):
                value = 2.0 * amps[i, j] - amps[j, i]
                mixed_ref[i, :, pl.ds(j * narrow, narrow)] = value.astype(BF)

    vmem = pl.BlockSpec(memory_space=pltpu.VMEM)
    return pl.pallas_call(
        body,
        out_shape=(
            jax.ShapeDtypeStruct((nocc, nocc, share // 2, narrow), F32),
            jax.ShapeDtypeStruct((nocc, nocc, share // 2, narrow), F32),
            jax.ShapeDtypeStruct((nocc, share, nocc * narrow), BF),
        ),
        in_specs=[pl.BlockSpec(memory_space=pltpu.SMEM), vmem, vmem, vmem],
        out_specs=(vmem, vmem, vmem),
        compiler_params=pltpu.CompilerParams(vmem_limit_bytes=12 * 1024 * 1024),
        name="amplitudes_of",
    )(slot, row_energy, col_energy, parts)


def place(value, nocc):
    nz, r, lanes = value.shape
    narrow = lanes // nocc
    nl = nz // 2

    def body(value_ref, out_ref):
        for i in range(nocc):
            for k in range(nz):
                block = (k % nl + nl // 2) % nl * 2 + k // nl
                out_ref[i, :, pl.ds(block * narrow, narrow)] = value_ref[k, :, pl.ds(i * narrow, narrow)]

    vmem = pl.BlockSpec(memory_space=pltpu.VMEM)
    return pl.pallas_call(
        body,
        out_shape=jax.ShapeDtypeStruct((nocc, r, nz * narrow), BF),
        in_specs=[vmem],
        out_specs=vmem,
        compiler_params=pltpu.CompilerParams(vmem_limit_bytes=12 * 1024 * 1024),
        name="place",
    )(value)


def local(half_ints, coef_virt, screen, occ_energy, virt_energy, batch_orbitals):
    p_rows, nocc, ao_part = half_ints.shape
    nv = virt_energy.shape[0]
    nx, nz, ny = lax.axis_size("x"), lax.axis_size("z"), lax.axis_size("y")
    nl = nz // 2
    x, z, c, y = (lax.axis_index(name) for name in ("x", "z", "c", "y"))
    zh, zl = z // nl, z % nl
    r = p_rows // ny
    wide = nv // nx
    narrow = nv // nz
    half = wide // 2
    share = half // ny
    ways = wide // narrow

    labels = jnp.arange(occ_energy.shape[0], dtype=jnp.int32)
    onehot = (batch_orbitals[:, None] == labels[None, :]).astype(F32)
    slot_energy = jnp.sum(onehot * occ_energy[None, :], axis=1)

    with jax.named_scope("transform"):
        copies = jnp.broadcast_to(coef_virt[None], (nz,) + coef_virt.shape)
        coef = exchange(copies, "z")
        expanded = jnp.repeat(jnp.repeat(screen, 32, axis=0), 128, axis=1).astype(BF)
        masked = half_ints * expanded[:, None, :]
        masked = masked.reshape(ny, r, nocc, ao_part).transpose(0, 2, 1, 3)
        masked = lax.all_gather(masked.reshape(-1, ao_part), "x", axis=0)
        masked = masked.reshape(nx, ny, nocc, r, ao_part)
        masked, coef = lax.optimization_barrier((masked, coef))
        low, high = by_core(coef, swap_cores(coef), c)
        coef = jnp.stack([low, high], axis=1).reshape(wide, ao_part)
        part = jnp.einsum("xyirm,am->yxira", masked, coef, preferred_element_type=F32)
        part = exchange(part.astype(BF).reshape(ny, nx * nocc * r, wide), "y")
        three = jnp.sum(part.astype(F32), axis=0).astype(BF).reshape(nx, nocc, r, wide)

    with jax.named_scope("panels"):
        row = jnp.concatenate([three[:, i] for i in range(nocc)], axis=-1)
        row = lax.all_gather(row.reshape(nx * r, nocc * wide), "z", axis=0, tiled=True)
        col = exchange(three.reshape(nx, nocc * r, wide), "x")
        col = jnp.roll(col, nx // 2, axis=0).reshape(nx, nocc, r, ways // 2, 2, narrow)
        col = jnp.concatenate(
            [col[:, i].transpose(3, 0, 2, 1, 4).reshape(nz, r, narrow) for i in range(nocc)], axis=-1
        )
        col = exchange(col, "z")
        col = lax.all_gather(col.reshape(nz * r, nocc * narrow), "x", axis=0)
        col = col.reshape(nx, nz, r, nocc * narrow)
        col = col.transpose(1, 0, 2, 3).reshape(nz * nx * r, nocc * narrow)

    with jax.named_scope("gram"):
        other = swap_cores(gram_half(row, col, 1 - c, nocc, ny))
        gram = gram_half(row, col, c, nocc, ny) + other
        gram = exchange(gram.astype(BF).reshape(ny, nocc * share, nocc * narrow), "y")

    with jax.named_scope("amplitudes"):
        row_energy = lax.dynamic_slice_in_dim(virt_energy, x * wide + c * half + y * share, share, 0)
        col_energy = lax.dynamic_slice_in_dim(virt_energy, ((zl + nl // 2) % nl * 2 + zh) * narrow, narrow, 0)
        upper, lower, mixed = amplitudes_of(gram, slot_energy, row_energy[:, None], col_energy[None, :])
        swap = []
        for h in range(2):
            for l in range(nl):
                for k in range(2):
                    swap.append(((h * nl + l) * 2 + k, (k * nl + (l + nl // 2) % nl) * 2 + h))
        upper = lax.ppermute(upper, ("z", "c"), swap)
        lower = lax.ppermute(lower, ("z", "c"), swap)
        mixed = lax.all_gather(mixed.reshape(nocc * share, nocc * narrow), "y", axis=0)
        mixed, upper = lax.optimization_barrier((mixed, upper))
        mixed = mixed.reshape(ny, nocc, share, nocc * narrow)
        theirs = swap_cores(mixed)

    with jax.named_scope("gamma"):
        value = contract(row, mixed, theirs, c, nx, nz)
        value = exchange(value.reshape(nx, nz * r, nocc * narrow), "x")
        value = jnp.sum(value.astype(F32), axis=0).astype(BF)
        value, lower = lax.optimization_barrier((value, lower))
        value = exchange(value.reshape(nz, r, nocc * narrow), "z")
        gamma = place(value, nocc)
    own = jnp.concatenate([upper, lower], axis=2)
    return own.transpose(0, 2, 1, 3)[None], gamma.transpose(1, 0, 2)


def solution(mesh):
    fine = Mesh(mesh.devices.reshape(4, mesh.shape["aux"] // 8, 2, mesh.shape["occ"]), ("x", "z", "c", "y"))
    aux = ("x", "z", "c")
    in_specs = (P(aux, None, "y"), P(aux, "y"), P(aux, "y"), P(), P(), P())
    out_specs = (P(aux, None, "y", None, None), P(aux + ("y",), None, None))
    return jax.shard_map(local, mesh=fine, in_specs=in_specs, out_specs=out_specs, check_vma=False)
```

```python
import jax
import jax.numpy as jnp
from jax import lax
from jax.experimental import pallas as pl
from jax.experimental.pallas import tpu as pltpu
from jax.sharding import Mesh
from jax.sharding import PartitionSpec as P

BF = jnp.bfloat16
F32 = jnp.float32


def swap_cores(value):
    return lax.ppermute(value, "c", [(0, 1), (1, 0)])


def exchange(value, axis):
    members, rows, lanes = value.shape
    value = value.reshape(members * rows, lanes)
    value = lax.all_to_all(value, axis, split_axis=0, concat_axis=0, tiled=True)
    return value.reshape(members, rows, lanes)


def by_core(mine, theirs, core):
    return jnp.where(core == 0, mine, theirs), jnp.where(core == 0, theirs, mine)


def gram_half(row, col, which, nocc, ny):
    k_rows, lanes = row.shape
    half = lanes // nocc // 2
    share = half // ny
    width = col.shape[1]

    def body(which_ref, row_ref, col_ref, out_ref):
        tile = lax.dot_general(
            row_ref[...], col_ref[...], (((0,), (0,)), ((), ())), preferred_element_type=F32
        )
        out_ref[...] = tile.reshape(ny, 1, share, width)

    return pl.pallas_call(
        body,
        out_shape=jax.ShapeDtypeStruct((ny, nocc, share, width), F32),
        grid_spec=pltpu.PrefetchScalarGridSpec(
            num_scalar_prefetch=1,
            grid=(nocc,),
            in_specs=[
                pl.BlockSpec((k_rows, half), lambda i, w: (0, 2 * i + w[0])),
                pl.BlockSpec((k_rows, width), lambda i, w: (0, 0)),
            ],
            out_specs=pl.BlockSpec((ny, 1, share, width), lambda i, w: (0, i, 0, 0)),
        ),
        compiler_params=pltpu.CompilerParams(vmem_limit_bytes=12 * 1024 * 1024),
        cost_estimate=pl.CostEstimate(
            flops=2 * k_rows * nocc * half * width,
            bytes_accessed=2 * k_rows * (nocc * half + width) + 4 * nocc * half * width,
            transcendentals=0,
        ),
        name="gram_half",
    )(which.reshape(1), row, col)


def contract(row, mine, theirs, core, nx, nz):
    k_rows, lanes = row.shape
    ny, nocc, share, width = mine.shape
    half = ny * share
    r = k_rows // nx // nz
    steps = 4
    zs = nz // steps

    def body(core_ref, row_ref, mine_ref, theirs_ref, out_ref, tile_ref):
        @pl.when(pl.program_id(0) == 0)
        def _():
            for i in range(nocc):
                for q in range(ny):
                    for k, ref in enumerate((mine_ref, theirs_ref)):
                        side = core_ref[0] if k == 0 else 1 - core_ref[0]
                        start = (2 * i + side) * half + q * share
                        tile_ref[pl.ds(pl.multiple_of(start, share), share), :] = ref[q, i]

        value = jnp.dot(row_ref[...], tile_ref[...], preferred_element_type=F32).astype(BF)
        value = value.reshape(zs, nx, r, width)
        for k in range(nx):
            out_ref[k] = value[:, k]

    return pl.pallas_call(
        body,
        out_shape=jax.ShapeDtypeStruct((nx, nz, r, width), BF),
        grid_spec=pltpu.PrefetchScalarGridSpec(
            num_scalar_prefetch=1,
            grid=(steps,),
            in_specs=[
                pl.BlockSpec((k_rows // steps, lanes), lambda s, w: (s, 0)),
                pl.BlockSpec((ny, nocc, share, width), lambda s, w: (0, 0, 0, 0)),
                pl.BlockSpec((ny, nocc, share, width), lambda s, w: (0, 0, 0, 0)),
            ],
            out_specs=pl.BlockSpec((nx, zs, r, width), lambda s, w: (0, s, 0, 0)),
            scratch_shapes=[pltpu.VMEM((lanes, width), BF)],
        ),
        compiler_params=pltpu.CompilerParams(vmem_limit_bytes=12 * 1024 * 1024),
        cost_estimate=pl.CostEstimate(
            flops=2 * k_rows * lanes * width,
            bytes_accessed=2 * k_rows * (lanes + width) + 2 * lanes * width,
            transcendentals=0,
        ),
        name="contract",
    )(core.reshape(1), row, mine, theirs)


def amplitudes_of(parts, slot, row_energy, col_energy):
    nocc = slot.shape[0]
    share, narrow = row_energy.shape[0], col_energy.shape[1]
    ways = parts.shape[0]

    def body(slot_ref, row_ref, col_ref, parts_ref, amps_ref, mixed_ref):
        amps = {}
        for i in range(nocc):
            for j in range(nocc):
                at = (pl.ds(i * share, share), pl.ds(j * narrow, narrow))
                total = parts_ref[(0,) + at].astype(F32)
                for k in range(1, ways):
                    total = total + parts_ref[(k,) + at].astype(F32)
                gap = slot_ref[i] + slot_ref[j] - row_ref[...] - col_ref[...]
                amps[i, j] = total / gap
                amps_ref[i, j] = amps[i, j].astype(BF)
        for i in range(nocc):
            for j in range(nocc):
                value = 2.0 * amps[i, j] - amps[j, i]
                mixed_ref[i, :, pl.ds(j * narrow, narrow)] = value.astype(BF)

    vmem = pl.BlockSpec(memory_space=pltpu.VMEM)
    return pl.pallas_call(
        body,
        out_shape=(
            jax.ShapeDtypeStruct((nocc, nocc, share, narrow), BF),
            jax.ShapeDtypeStruct((nocc, share, nocc * narrow), BF),
        ),
        in_specs=[pl.BlockSpec(memory_space=pltpu.SMEM), vmem, vmem, vmem],
        out_specs=(vmem, vmem),
        compiler_params=pltpu.CompilerParams(vmem_limit_bytes=12 * 1024 * 1024),
        name="amplitudes_of",
    )(slot, row_energy, col_energy, parts)


def place(value, nocc):
    nz, r, lanes = value.shape
    narrow = lanes // nocc
    nl = nz // 2

    def body(value_ref, out_ref):
        for i in range(nocc):
            for k in range(nz):
                block = (k % nl + nl // 2) % nl * 2 + k // nl
                out_ref[i, :, pl.ds(block * narrow, narrow)] = value_ref[k, :, pl.ds(i * narrow, narrow)]

    vmem = pl.BlockSpec(memory_space=pltpu.VMEM)
    return pl.pallas_call(
        body,
        out_shape=jax.ShapeDtypeStruct((nocc, r, nz * narrow), BF),
        in_specs=[vmem],
        out_specs=vmem,
        compiler_params=pltpu.CompilerParams(vmem_limit_bytes=12 * 1024 * 1024),
        name="place",
    )(value)


def local(half_ints, coef_virt, screen, occ_energy, virt_energy, batch_orbitals):
    p_rows, nocc, ao_part = half_ints.shape
    nv = virt_energy.shape[0]
    nx, nz, ny = lax.axis_size("x"), lax.axis_size("z"), lax.axis_size("y")
    nl = nz // 2
    x, z, c, y = (lax.axis_index(name) for name in ("x", "z", "c", "y"))
    zh, zl = z // nl, z % nl
    r = p_rows // ny
    wide = nv // nx
    narrow = nv // nz
    half = wide // 2
    share = half // ny
    ways = wide // narrow

    labels = jnp.arange(occ_energy.shape[0], dtype=jnp.int32)
    onehot = (batch_orbitals[:, None] == labels[None, :]).astype(F32)
    slot_energy = jnp.sum(onehot * occ_energy[None, :], axis=1)

    with jax.named_scope("transform"):
        copies = jnp.broadcast_to(coef_virt[None], (nz,) + coef_virt.shape)
        coef = exchange(copies, "z")
        expanded = jnp.repeat(jnp.repeat(screen, 32, axis=0), 128, axis=1).astype(BF)
        masked = half_ints * expanded[:, None, :]
        masked = masked.reshape(ny, r, nocc, ao_part).transpose(0, 2, 1, 3)
        masked = lax.all_gather(masked.reshape(-1, ao_part), "x", axis=0)
        masked = masked.reshape(nx, ny, nocc, r, ao_part)
        masked, coef = lax.optimization_barrier((masked, coef))
        low, high = by_core(coef, swap_cores(coef), c)
        coef = jnp.stack([low, high], axis=1).reshape(wide, ao_part)
        part = jnp.einsum("xyirm,am->yxira", masked, coef, preferred_element_type=F32)
        part = exchange(part.astype(BF).reshape(ny, nx * nocc * r, wide), "y")
        three = jnp.sum(part.astype(F32), axis=0).astype(BF).reshape(nx, nocc, r, wide)

    with jax.named_scope("panels"):
        row = jnp.concatenate([three[:, i] for i in range(nocc)], axis=-1)
        row = lax.all_gather(row.reshape(nx * r, nocc * wide), "z", axis=0, tiled=True)
        col = exchange(three.reshape(nx, nocc * r, wide), "x")
        col = jnp.roll(col, nx // 2, axis=0).reshape(nx, nocc, r, ways // 2, 2, narrow)
        col = jnp.concatenate(
            [col[:, i].transpose(3, 0, 2, 1, 4).reshape(nz, r, narrow) for i in range(nocc)], axis=-1
        )
        col = exchange(col, "z")
        col = lax.all_gather(col.reshape(nz * r, nocc * narrow), "x", axis=0)
        col = col.reshape(nx, nz, r, nocc * narrow)
        col = col.transpose(1, 0, 2, 3).reshape(nz * nx * r, nocc * narrow)

    with jax.named_scope("gram"):
        other = swap_cores(gram_half(row, col, 1 - c, nocc, ny))
        gram = gram_half(row, col, c, nocc, ny) + other
        gram = exchange(gram.astype(BF).reshape(ny, nocc * share, nocc * narrow), "y")

    with jax.named_scope("amplitudes"):
        row_energy = lax.dynamic_slice_in_dim(virt_energy, x * wide + c * half + y * share, share, 0)
        col_energy = lax.dynamic_slice_in_dim(virt_energy, ((zl + nl // 2) % nl * 2 + zh) * narrow, narrow, 0)
        amps, mixed = amplitudes_of(gram, slot_energy, row_energy[:, None], col_energy[None, :])
        swap = []
        for h in range(2):
            for l in range(nl):
                for k in range(2):
                    swap.append(((h * nl + l) * 2 + k, (k * nl + (l + nl // 2) % nl) * 2 + h))
        own = lax.ppermute(amps, ("z", "c"), swap)
        mixed = lax.all_gather(mixed.reshape(nocc * share, nocc * narrow), "y", axis=0)
        mixed = mixed.reshape(ny, nocc, share, nocc * narrow)
        theirs = swap_cores(mixed)

    with jax.named_scope("gamma"):
        value = contract(row, mixed, theirs, c, nx, nz)
        value = exchange(value.reshape(nx, nz * r, nocc * narrow), "x")
        value = jnp.sum(value.astype(F32), axis=0).astype(BF)
        value, own = lax.optimization_barrier((value, own))
        value = exchange(value.reshape(nz, r, nocc * narrow), "z")
        gamma = place(value, nocc)
    return own.astype(F32).transpose(0, 2, 1, 3)[None], gamma.transpose(1, 0, 2)


def solution(mesh):
    fine = Mesh(mesh.devices.reshape(4, mesh.shape["aux"] // 8, 2, mesh.shape["occ"]), ("x", "z", "c", "y"))
    aux = ("x", "z", "c")
    in_specs = (P(aux, None, "y"), P(aux, "y"), P(aux, "y"), P(), P(), P())
    out_specs = (P(aux, None, "y", None, None), P(aux + ("y",), None, None))
    return jax.shard_map(local, mesh=fine, in_specs=in_specs, out_specs=out_specs, check_vma=False)
```

```python
import jax
import jax.numpy as jnp
from jax import lax
from jax.experimental import pallas as pl
from jax.experimental.pallas import tpu as pltpu
from jax.sharding import Mesh
from jax.sharding import PartitionSpec as P

BF = jnp.bfloat16
F32 = jnp.float32


def swap_cores(value):
    return lax.ppermute(value, "c", [(0, 1), (1, 0)])


def exchange(value, axis):
    members, rows, lanes = value.shape
    value = value.reshape(members * rows, lanes)
    value = lax.all_to_all(value, axis, split_axis=0, concat_axis=0, tiled=True)
    return value.reshape(members, rows, lanes)


def by_core(mine, theirs, core):
    return jnp.where(core == 0, mine, theirs), jnp.where(core == 0, theirs, mine)


def gram_half(row, col, which, nocc, ny, room):
    k_rows, lanes = row.shape
    half = lanes // nocc // 2
    share = half // ny
    nx, nz, r, width = col.shape

    def body(which_ref, row_ref, col_ref, out_ref, order_ref):
        @pl.when(pl.program_id(0) == 0)
        def _():
            for k in range(nz):
                for m in range(nx):
                    order_ref[(k * nx + m) * r : (k * nx + m + 1) * r, :] = col_ref[m, k]

        tile = lax.dot_general(
            row_ref[...], order_ref[...], (((0,), (0,)), ((), ())), preferred_element_type=F32
        )
        out_ref[...] = tile.reshape(ny, 1, share, width)

    return pl.pallas_call(
        body,
        out_shape=jax.ShapeDtypeStruct((ny, nocc, share, width), F32),
        grid_spec=pltpu.PrefetchScalarGridSpec(
            num_scalar_prefetch=1,
            grid=(nocc,),
            in_specs=[
                pl.BlockSpec((k_rows, half), lambda i, w: (0, 2 * i + w[0])),
                pl.BlockSpec((nx, nz, r, width), lambda i, w: (0, 0, 0, 0)),
            ],
            out_specs=pl.BlockSpec((ny, 1, share, width), lambda i, w: (0, i, 0, 0)),
            scratch_shapes=[pltpu.VMEM((k_rows, width), BF)],
        ),
        compiler_params=pltpu.CompilerParams(vmem_limit_bytes=room * 1024 * 1024),
        cost_estimate=pl.CostEstimate(
            flops=2 * k_rows * nocc * half * width,
            bytes_accessed=2 * k_rows * (nocc * half + width) + 4 * nocc * half * width,
            transcendentals=0,
        ),
        name="gram_half",
    )(which.reshape(1), row, col)


def contract(row, mine, theirs, core, nx, nz):
    k_rows, lanes = row.shape
    ny, nocc, share, width = mine.shape
    half = ny * share
    r = k_rows // nx // nz
    steps = 4
    zs = nz // steps

    def body(core_ref, row_ref, mine_ref, theirs_ref, out_ref, tile_ref):
        @pl.when(pl.program_id(0) == 0)
        def _():
            for i in range(nocc):
                for q in range(ny):
                    for k, ref in enumerate((mine_ref, theirs_ref)):
                        side = core_ref[0] if k == 0 else 1 - core_ref[0]
                        start = (2 * i + side) * half + q * share
                        tile_ref[pl.ds(pl.multiple_of(start, share), share), :] = ref[q, i]

        value = jnp.dot(row_ref[...], tile_ref[...], preferred_element_type=F32).astype(BF)
        value = value.reshape(zs, nx, r, width)
        for k in range(nx):
            out_ref[k] = value[:, k]

    return pl.pallas_call(
        body,
        out_shape=jax.ShapeDtypeStruct((nx, nz, r, width), BF),
        grid_spec=pltpu.PrefetchScalarGridSpec(
            num_scalar_prefetch=1,
            grid=(steps,),
            in_specs=[
                pl.BlockSpec((k_rows // steps, lanes), lambda s, w: (s, 0)),
                pl.BlockSpec((ny, nocc, share, width), lambda s, w: (0, 0, 0, 0)),
                pl.BlockSpec((ny, nocc, share, width), lambda s, w: (0, 0, 0, 0)),
            ],
            out_specs=pl.BlockSpec((nx, zs, r, width), lambda s, w: (0, s, 0, 0)),
            scratch_shapes=[pltpu.VMEM((lanes, width), BF)],
        ),
        compiler_params=pltpu.CompilerParams(vmem_limit_bytes=12 * 1024 * 1024),
        cost_estimate=pl.CostEstimate(
            flops=2 * k_rows * lanes * width,
            bytes_accessed=2 * k_rows * (lanes + width) + 2 * lanes * width,
            transcendentals=0,
        ),
        name="contract",
    )(core.reshape(1), row, mine, theirs)


def amplitudes_of(parts, slot, row_energy, col_energy):
    nocc = slot.shape[0]
    share, narrow = row_energy.shape[0], col_energy.shape[1]
    ways = parts.shape[0]

    def body(slot_ref, row_ref, col_ref, parts_ref, amps_ref, mixed_ref):
        amps = {}
        for i in range(nocc):
            for j in range(nocc):
                at = (pl.ds(i * share, share), pl.ds(j * narrow, narrow))
                total = parts_ref[(0,) + at].astype(F32)
                for k in range(1, ways):
                    total = total + parts_ref[(k,) + at].astype(F32)
                gap = slot_ref[i] + slot_ref[j] - row_ref[...] - col_ref[...]
                amps[i, j] = total / gap
                amps_ref[i, j] = amps[i, j].astype(BF)
        for i in range(nocc):
            for j in range(nocc):
                value = 2.0 * amps[i, j] - amps[j, i]
                mixed_ref[i, :, pl.ds(j * narrow, narrow)] = value.astype(BF)

    vmem = pl.BlockSpec(memory_space=pltpu.VMEM)
    return pl.pallas_call(
        body,
        out_shape=(
            jax.ShapeDtypeStruct((nocc, nocc, share, narrow), BF),
            jax.ShapeDtypeStruct((nocc, share, nocc * narrow), BF),
        ),
        in_specs=[pl.BlockSpec(memory_space=pltpu.SMEM), vmem, vmem, vmem],
        out_specs=(vmem, vmem),
        compiler_params=pltpu.CompilerParams(vmem_limit_bytes=12 * 1024 * 1024),
        name="amplitudes_of",
    )(slot, row_energy, col_energy, parts)


def place(value, nocc):
    nz, r, lanes = value.shape
    narrow = lanes // nocc
    nl = nz // 2

    def body(value_ref, out_ref):
        for i in range(nocc):
            for k in range(nz):
                block = (k % nl + nl // 2) % nl * 2 + k // nl
                out_ref[i, :, pl.ds(block * narrow, narrow)] = value_ref[k, :, pl.ds(i * narrow, narrow)]

    vmem = pl.BlockSpec(memory_space=pltpu.VMEM)
    return pl.pallas_call(
        body,
        out_shape=jax.ShapeDtypeStruct((nocc, r, nz * narrow), BF),
        in_specs=[vmem],
        out_specs=vmem,
        compiler_params=pltpu.CompilerParams(vmem_limit_bytes=12 * 1024 * 1024),
        name="place",
    )(value)


def local(half_ints, coef_virt, screen, occ_energy, virt_energy, batch_orbitals):
    p_rows, nocc, ao_part = half_ints.shape
    nv = virt_energy.shape[0]
    nx, nz, ny = lax.axis_size("x"), lax.axis_size("z"), lax.axis_size("y")
    nl = nz // 2
    x, z, c, y = (lax.axis_index(name) for name in ("x", "z", "c", "y"))
    zh, zl = z // nl, z % nl
    r = p_rows // ny
    wide = nv // nx
    narrow = nv // nz
    half = wide // 2
    share = half // ny
    ways = wide // narrow

    labels = jnp.arange(occ_energy.shape[0], dtype=jnp.int32)
    onehot = (batch_orbitals[:, None] == labels[None, :]).astype(F32)
    slot_energy = jnp.sum(onehot * occ_energy[None, :], axis=1)

    with jax.named_scope("transform"):
        copies = jnp.broadcast_to(coef_virt[None], (nz,) + coef_virt.shape)
        coef = exchange(copies, "z")
        expanded = jnp.repeat(jnp.repeat(screen, 32, axis=0), 128, axis=1).astype(BF)
        masked = half_ints * expanded[:, None, :]
        masked = masked.reshape(ny, r, nocc, ao_part).transpose(0, 2, 1, 3)
        masked = lax.all_gather(masked.reshape(-1, ao_part), "x", axis=0)
        masked = masked.reshape(nx, ny, nocc, r, ao_part)
        masked, coef = lax.optimization_barrier((masked, coef))
        low, high = by_core(coef, swap_cores(coef), c)
        coef = jnp.stack([low, high], axis=1).reshape(wide, ao_part)
        part = jnp.einsum("xyirm,am->yxira", masked, coef, preferred_element_type=F32)
        part = exchange(part.astype(BF).reshape(ny, nx * nocc * r, wide), "y")
        three = jnp.sum(part.astype(F32), axis=0).astype(BF).reshape(nx, nocc, r, wide)

    with jax.named_scope("panels"):
        row = jnp.concatenate([three[:, i] for i in range(nocc)], axis=-1)
        row = lax.all_gather(row.reshape(nx * r, nocc * wide), "z", axis=0, tiled=True)
        col = exchange(three.reshape(nx, nocc * r, wide), "x")
        col = jnp.roll(col, nx // 2, axis=0).reshape(nx, nocc, r, ways // 2, 2, narrow)
        col = jnp.concatenate(
            [col[:, i].transpose(3, 0, 2, 1, 4).reshape(nz, r, narrow) for i in range(nocc)], axis=-1
        )
        col = exchange(col, "z")
        col = lax.all_gather(col.reshape(nz * r, nocc * narrow), "x", axis=0)
        col = col.reshape(nx, nz, r, nocc * narrow)

    with jax.named_scope("gram"):
        other = swap_cores(gram_half(row, col, 1 - c, nocc, ny, 58))
        gram = gram_half(row, col, c, nocc, ny, 12) + other
        gram = exchange(gram.astype(BF).reshape(ny, nocc * share, nocc * narrow), "y")

    with jax.named_scope("amplitudes"):
        row_energy = lax.dynamic_slice_in_dim(virt_energy, x * wide + c * half + y * share, share, 0)
        col_energy = lax.dynamic_slice_in_dim(virt_energy, ((zl + nl // 2) % nl * 2 + zh) * narrow, narrow, 0)
        amps, mixed = amplitudes_of(gram, slot_energy, row_energy[:, None], col_energy[None, :])
        swap = []
        for h in range(2):
            for l in range(nl):
                for k in range(2):
                    swap.append(((h * nl + l) * 2 + k, (k * nl + (l + nl // 2) % nl) * 2 + h))
        own = lax.ppermute(amps, ("z", "c"), swap)
        mixed = lax.all_gather(mixed.reshape(nocc * share, nocc * narrow), "y", axis=0)
        mixed = mixed.reshape(ny, nocc, share, nocc * narrow)
        theirs = swap_cores(mixed)

    with jax.named_scope("gamma"):
        value = contract(row, mixed, theirs, c, nx, nz)
        value = exchange(value.reshape(nx, nz * r, nocc * narrow), "x")
        value = jnp.sum(value.astype(F32), axis=0).astype(BF)
        value, own = lax.optimization_barrier((value, own))
        value = exchange(value.reshape(nz, r, nocc * narrow), "z")
        gamma = place(value, nocc)
    return own.astype(F32).transpose(0, 2, 1, 3)[None], gamma.transpose(1, 0, 2)


def solution(mesh):
    fine = Mesh(mesh.devices.reshape(4, mesh.shape["aux"] // 8, 2, mesh.shape["occ"]), ("x", "z", "c", "y"))
    aux = ("x", "z", "c")
    in_specs = (P(aux, None, "y"), P(aux, "y"), P(aux, "y"), P(), P(), P())
    out_specs = (P(aux, None, "y", None, None), P(aux + ("y",), None, None))
    return jax.shard_map(local, mesh=fine, in_specs=in_specs, out_specs=out_specs, check_vma=False)
```

```python
import jax
import jax.numpy as jnp
from jax import lax
from jax.experimental import pallas as pl
from jax.experimental.pallas import tpu as pltpu
from jax.sharding import Mesh
from jax.sharding import PartitionSpec as P

BF = jnp.bfloat16
F32 = jnp.float32


def swap_cores(value):
    return lax.ppermute(value, "c", [(0, 1), (1, 0)])


def exchange(value, axis):
    members, rows, lanes = value.shape
    value = value.reshape(members * rows, lanes)
    value = lax.all_to_all(value, axis, split_axis=0, concat_axis=0, tiled=True)
    return value.reshape(members, rows, lanes)


def by_core(mine, theirs, core):
    return jnp.where(core == 0, mine, theirs), jnp.where(core == 0, theirs, mine)


def gram_half(row, col, which, nocc, ny, kind):
    k_rows, lanes = row.shape
    half = lanes // nocc // 2
    share = half // ny
    nx, nz, r, width = col.shape

    def body(which_ref, row_ref, col_ref, out_ref, order_ref):
        @pl.when(pl.program_id(0) == 0)
        def _():
            for k in range(nz):
                for m in range(nx):
                    order_ref[(k * nx + m) * r : (k * nx + m + 1) * r, :] = col_ref[m, k]

        tile = lax.dot_general(
            row_ref[...], order_ref[...], (((0,), (0,)), ((), ())), preferred_element_type=F32
        )
        out_ref[...] = tile.reshape(ny, 1, share, width).astype(kind)

    return pl.pallas_call(
        body,
        out_shape=jax.ShapeDtypeStruct((ny, nocc, share, width), kind),
        grid_spec=pltpu.PrefetchScalarGridSpec(
            num_scalar_prefetch=1,
            grid=(nocc,),
            in_specs=[
                pl.BlockSpec((k_rows, half), lambda i, w: (0, 2 * i + w[0])),
                pl.BlockSpec((nx, nz, r, width), lambda i, w: (0, 0, 0, 0)),
            ],
            out_specs=pl.BlockSpec((ny, 1, share, width), lambda i, w: (0, i, 0, 0)),
            scratch_shapes=[pltpu.VMEM((k_rows, width), BF)],
        ),
        compiler_params=pltpu.CompilerParams(vmem_limit_bytes=12 * 1024 * 1024),
        cost_estimate=pl.CostEstimate(
            flops=2 * k_rows * nocc * half * width,
            bytes_accessed=2 * k_rows * (nocc * half + width) + 4 * nocc * half * width,
            transcendentals=0,
        ),
        name="gram_half",
    )(which.reshape(1), row, col)


def contract(row, tile, side, nx, nz, base=None):
    k_rows, lanes = row.shape
    ny, nocc, share, width = tile.shape
    half = ny * share
    r = k_rows // nx // nz
    steps = 4
    zs = nz // steps
    size = k_rows // steps

    def body(side_ref, *refs):
        rows, tile_ref, rest = refs[:nocc], refs[nocc], refs[nocc + 1 :]
        total = jnp.zeros((size, width), F32) if base is None else rest[0][...]
        for i in range(nocc):
            total = total + jnp.dot(
                rows[i][...], tile_ref[:, i].reshape(half, width), preferred_element_type=F32
            )
        if base is None:
            rest[-1][...] = total
        else:
            value = total.astype(BF).reshape(zs, nx, r, width)
            for k in range(nx):
                rest[-1][k] = value[:, k]

    def lane_block(i):
        return pl.BlockSpec((size, half), lambda s, w: (s, 2 * i + w[0]))

    flat = pl.BlockSpec((size, width), lambda s, w: (s, 0))
    in_specs = [lane_block(i) for i in range(nocc)]
    in_specs.append(pl.BlockSpec((ny, nocc, share, width), lambda s, w: (0, 0, 0, 0)))
    if base is None:
        out_shape, out_specs, extra = jax.ShapeDtypeStruct((k_rows, width), F32), flat, ()
    else:
        in_specs.append(flat)
        out_shape = jax.ShapeDtypeStruct((nx, nz, r, width), BF)
        out_specs, extra = pl.BlockSpec((nx, zs, r, width), lambda s, w: (0, s, 0, 0)), (base,)
    return pl.pallas_call(
        body,
        out_shape=out_shape,
        grid_spec=pltpu.PrefetchScalarGridSpec(
            num_scalar_prefetch=1, grid=(steps,), in_specs=in_specs, out_specs=out_specs
        ),
        compiler_params=pltpu.CompilerParams(vmem_limit_bytes=12 * 1024 * 1024),
        cost_estimate=pl.CostEstimate(
            flops=k_rows * lanes * width,
            bytes_accessed=k_rows * (lanes + 4 * width) + lanes * width,
            transcendentals=0,
        ),
        name="contract",
    )(side.reshape(1), *([row] * nocc), tile, *extra)


def amplitudes_of(parts, slot, row_energy, col_energy):
    nocc = slot.shape[0]
    share, narrow = row_energy.shape[0], col_energy.shape[1]
    ways = parts.shape[0]

    def body(slot_ref, row_ref, col_ref, parts_ref, amps_ref, mixed_ref):
        amps = {}
        for i in range(nocc):
            for j in range(nocc):
                at = (pl.ds(i * share, share), pl.ds(j * narrow, narrow))
                total = parts_ref[(0,) + at].astype(F32)
                for k in range(1, ways):
                    total = total + parts_ref[(k,) + at].astype(F32)
                gap = slot_ref[i] + slot_ref[j] - row_ref[...] - col_ref[...]
                amps[i, j] = total / gap
                amps_ref[i, j] = amps[i, j].astype(BF)
        for i in range(nocc):
            for j in range(nocc):
                value = 2.0 * amps[i, j] - amps[j, i]
                mixed_ref[i, :, pl.ds(j * narrow, narrow)] = value.astype(BF)

    vmem = pl.BlockSpec(memory_space=pltpu.VMEM)
    return pl.pallas_call(
        body,
        out_shape=(
            jax.ShapeDtypeStruct((nocc, nocc, share, narrow), BF),
            jax.ShapeDtypeStruct((nocc, share, nocc * narrow), BF),
        ),
        in_specs=[pl.BlockSpec(memory_space=pltpu.SMEM), vmem, vmem, vmem],
        out_specs=(vmem, vmem),
        compiler_params=pltpu.CompilerParams(vmem_limit_bytes=12 * 1024 * 1024),
        name="amplitudes_of",
    )(slot, row_energy, col_energy, parts)


def place(value, nocc):
    nz, r, lanes = value.shape
    narrow = lanes // nocc
    nl = nz // 2

    def body(value_ref, out_ref):
        for i in range(nocc):
            for k in range(nz):
                block = (k % nl + nl // 2) % nl * 2 + k // nl
                out_ref[i, :, pl.ds(block * narrow, narrow)] = value_ref[k, :, pl.ds(i * narrow, narrow)]

    vmem = pl.BlockSpec(memory_space=pltpu.VMEM)
    return pl.pallas_call(
        body,
        out_shape=jax.ShapeDtypeStruct((nocc, r, nz * narrow), BF),
        in_specs=[vmem],
        out_specs=vmem,
        compiler_params=pltpu.CompilerParams(vmem_limit_bytes=12 * 1024 * 1024),
        name="place",
    )(value)


def local(half_ints, coef_virt, screen, occ_energy, virt_energy, batch_orbitals):
    p_rows, nocc, ao_part = half_ints.shape
    nv = virt_energy.shape[0]
    nx, nz, ny = lax.axis_size("x"), lax.axis_size("z"), lax.axis_size("y")
    nl = nz // 2
    x, z, c, y = (lax.axis_index(name) for name in ("x", "z", "c", "y"))
    zh, zl = z // nl, z % nl
    r = p_rows // ny
    wide = nv // nx
    narrow = nv // nz
    half = wide // 2
    share = half // ny
    ways = wide // narrow

    labels = jnp.arange(occ_energy.shape[0], dtype=jnp.int32)
    onehot = (batch_orbitals[:, None] == labels[None, :]).astype(F32)
    slot_energy = jnp.sum(onehot * occ_energy[None, :], axis=1)

    with jax.named_scope("transform"):
        copies = jnp.broadcast_to(coef_virt[None], (nz,) + coef_virt.shape)
        coef = exchange(copies, "z")
        expanded = jnp.repeat(jnp.repeat(screen, 32, axis=0), 128, axis=1).astype(BF)
        masked = half_ints * expanded[:, None, :]
        masked = masked.reshape(ny, r, nocc, ao_part).transpose(0, 2, 1, 3)
        masked = lax.all_gather(masked.reshape(-1, ao_part), "x", axis=0)
        masked = masked.reshape(nx, ny, nocc, r, ao_part)
        masked, coef = lax.optimization_barrier((masked, coef))
        low, high = by_core(coef, swap_cores(coef), c)
        coef = jnp.stack([low, high], axis=1).reshape(wide, ao_part)
        part = jnp.einsum("xyirm,am->yxira", masked, coef, preferred_element_type=F32)
        part = exchange(part.astype(BF).reshape(ny, nx * nocc * r, wide), "y")
        three = jnp.sum(part.astype(F32), axis=0).astype(BF).reshape(nx, nocc, r, wide)

    with jax.named_scope("panels"):
        row = jnp.concatenate([three[:, i] for i in range(nocc)], axis=-1)
        row = lax.all_gather(row.reshape(nx * r, nocc * wide), "z", axis=0, tiled=True)
        col = exchange(three.reshape(nx, nocc * r, wide), "x")
        col = jnp.roll(col, nx // 2, axis=0).reshape(nx, nocc, r, ways // 2, 2, narrow)
        col = jnp.concatenate(
            [col[:, i].transpose(3, 0, 2, 1, 4).reshape(nz, r, narrow) for i in range(nocc)], axis=-1
        )
        col = exchange(col, "z")
        col = lax.all_gather(col.reshape(nz * r, nocc * narrow), "x", axis=0)
        col = col.reshape(nx, nz, r, nocc * narrow)

    with jax.named_scope("gram"):
        other = swap_cores(gram_half(row, col, 1 - c, nocc, ny, BF))
        gram = gram_half(row, col, c, nocc, ny, F32) + other.astype(F32)
        gram = exchange(gram.astype(BF).reshape(ny, nocc * share, nocc * narrow), "y")

    with jax.named_scope("amplitudes"):
        row_energy = lax.dynamic_slice_in_dim(virt_energy, x * wide + c * half + y * share, share, 0)
        col_energy = lax.dynamic_slice_in_dim(virt_energy, ((zl + nl // 2) % nl * 2 + zh) * narrow, narrow, 0)
        amps, mixed = amplitudes_of(gram, slot_energy, row_energy[:, None], col_energy[None, :])
        swap = []
        for h in range(2):
            for l in range(nl):
                for k in range(2):
                    swap.append(((h * nl + l) * 2 + k, (k * nl + (l + nl // 2) % nl) * 2 + h))
        own = lax.ppermute(amps, ("z", "c"), swap)
        mixed = lax.all_gather(mixed.reshape(nocc * share, nocc * narrow), "y", axis=0)
        mixed = mixed.reshape(ny, nocc, share, nocc * narrow)
        theirs = swap_cores(mixed)

    with jax.named_scope("gamma"):
        value = contract(row, theirs, 1 - c, nx, nz, contract(row, mixed, c, nx, nz))
        value = exchange(value.reshape(nx, nz * r, nocc * narrow), "x")
        value = jnp.sum(value.astype(F32), axis=0).astype(BF)
        value, own = lax.optimization_barrier((value, own))
        value = exchange(value.reshape(nz, r, nocc * narrow), "z")
        gamma = place(value, nocc)
    return own.astype(F32).transpose(0, 2, 1, 3)[None], gamma.transpose(1, 0, 2)


def solution(mesh):
    fine = Mesh(mesh.devices.reshape(4, mesh.shape["aux"] // 8, 2, mesh.shape["occ"]), ("x", "z", "c", "y"))
    aux = ("x", "z", "c")
    in_specs = (P(aux, None, "y"), P(aux, "y"), P(aux, "y"), P(), P(), P())
    out_specs = (P(aux, None, "y", None, None), P(aux + ("y",), None, None))
    return jax.shard_map(local, mesh=fine, in_specs=in_specs, out_specs=out_specs, check_vma=False)
```

```python
import jax
import jax.numpy as jnp
from jax import lax
from jax.experimental import pallas as pl
from jax.experimental.pallas import tpu as pltpu
from jax.sharding import Mesh
from jax.sharding import PartitionSpec as P

BF = jnp.bfloat16
F32 = jnp.float32


def swap_cores(value):
    return lax.ppermute(value, "c", [(0, 1), (1, 0)])


def exchange(value, axis):
    members, rows, lanes = value.shape
    value = value.reshape(members * rows, lanes)
    value = lax.all_to_all(value, axis, split_axis=0, concat_axis=0, tiled=True)
    return value.reshape(members, rows, lanes)


def by_core(mine, theirs, core):
    return jnp.where(core == 0, mine, theirs), jnp.where(core == 0, theirs, mine)


def spread(value, copies):
    def body(value_ref, out_ref, sems):
        moves = [pltpu.make_async_copy(value_ref, out_ref.at[k], sems.at[k]) for k in range(copies)]
        for move in moves:
            move.start()
        for move in moves:
            move.wait()

    return pl.pallas_call(
        body,
        out_shape=pltpu.HBM((copies,) + value.shape, value.dtype),
        in_specs=[pl.BlockSpec(memory_space=pltpu.VMEM)],
        out_specs=pl.BlockSpec(memory_space=pltpu.HBM),
        scratch_shapes=[pltpu.SemaphoreType.DMA((copies,))],
        compiler_params=pltpu.CompilerParams(vmem_limit_bytes=12 * 1024 * 1024),
        name="spread",
    )(value)


def gram_half(row, col, which, nocc, ny, kind):
    k_rows, lanes = row.shape
    half = lanes // nocc // 2
    share = half // ny
    nx, nz, r, width = col.shape

    def body(which_ref, row_ref, col_ref, out_ref, order_ref):
        @pl.when(pl.program_id(0) == 0)
        def _():
            for k in range(nz):
                for m in range(nx):
                    order_ref[(k * nx + m) * r : (k * nx + m + 1) * r, :] = col_ref[m, k]

        tile = lax.dot_general(
            row_ref[...], order_ref[...], (((0,), (0,)), ((), ())), preferred_element_type=F32
        )
        out_ref[...] = tile.reshape(ny, 1, share, width).astype(kind)

    return pl.pallas_call(
        body,
        out_shape=jax.ShapeDtypeStruct((ny, nocc, share, width), kind),
        grid_spec=pltpu.PrefetchScalarGridSpec(
            num_scalar_prefetch=1,
            grid=(nocc,),
            in_specs=[
                pl.BlockSpec((k_rows, half), lambda i, w: (0, 2 * i + w[0])),
                pl.BlockSpec((nx, nz, r, width), lambda i, w: (0, 0, 0, 0)),
            ],
            out_specs=pl.BlockSpec((ny, 1, share, width), lambda i, w: (0, i, 0, 0)),
            scratch_shapes=[pltpu.VMEM((k_rows, width), BF)],
        ),
        compiler_params=pltpu.CompilerParams(vmem_limit_bytes=12 * 1024 * 1024),
        cost_estimate=pl.CostEstimate(
            flops=2 * k_rows * nocc * half * width,
            bytes_accessed=2 * k_rows * (nocc * half + width) + 4 * nocc * half * width,
            transcendentals=0,
        ),
        name="gram_half",
    )(which.reshape(1), row, col)


def contract(row, tile, side, nx, nz, base=None):
    k_rows, lanes = row.shape
    ny, nocc, share, width = tile.shape
    half = ny * share
    r = k_rows // nx // nz
    steps = 4
    zs = nz // steps
    size = k_rows // steps

    def body(side_ref, *refs):
        rows, tile_ref, rest = refs[:nocc], refs[nocc], refs[nocc + 1 :]
        total = jnp.zeros((size, width), F32) if base is None else rest[0][...]
        for i in range(nocc):
            total = total + jnp.dot(
                rows[i][...], tile_ref[:, i].reshape(half, width), preferred_element_type=F32
            )
        if base is None:
            rest[-1][...] = total
        else:
            value = total.astype(BF).reshape(zs, nx, r, width)
            for k in range(nx):
                rest[-1][k] = value[:, k]

    def lane_block(i):
        return pl.BlockSpec((size, half), lambda s, w: (s, 2 * i + w[0]))

    flat = pl.BlockSpec((size, width), lambda s, w: (s, 0))
    in_specs = [lane_block(i) for i in range(nocc)]
    in_specs.append(pl.BlockSpec((ny, nocc, share, width), lambda s, w: (0, 0, 0, 0)))
    if base is None:
        out_shape, out_specs, extra = jax.ShapeDtypeStruct((k_rows, width), F32), flat, ()
    else:
        in_specs.append(flat)
        out_shape = pltpu.HBM((nx, nz, r, width), BF)
        out_specs, extra = pl.BlockSpec((nx, zs, r, width), lambda s, w: (0, s, 0, 0)), (base,)
    return pl.pallas_call(
        body,
        out_shape=out_shape,
        grid_spec=pltpu.PrefetchScalarGridSpec(
            num_scalar_prefetch=1, grid=(steps,), in_specs=in_specs, out_specs=out_specs
        ),
        compiler_params=pltpu.CompilerParams(vmem_limit_bytes=12 * 1024 * 1024),
        cost_estimate=pl.CostEstimate(
            flops=k_rows * lanes * width,
            bytes_accessed=k_rows * (lanes + 4 * width) + lanes * width,
            transcendentals=0,
        ),
        name="contract",
    )(side.reshape(1), *([row] * nocc), tile, *extra)


def amplitudes_of(parts, slot, row_energy, col_energy):
    nocc = slot.shape[0]
    share, narrow = row_energy.shape[0], col_energy.shape[1]
    ways = parts.shape[0]

    def body(slot_ref, row_ref, col_ref, parts_ref, amps_ref, mixed_ref):
        amps = {}
        for i in range(nocc):
            for j in range(nocc):
                at = (pl.ds(i * share, share), pl.ds(j * narrow, narrow))
                total = parts_ref[(0,) + at].astype(F32)
                for k in range(1, ways):
                    total = total + parts_ref[(k,) + at].astype(F32)
                gap = slot_ref[i] + slot_ref[j] - row_ref[...] - col_ref[...]
                amps[i, j] = total / gap
                amps_ref[i, j] = amps[i, j].astype(BF)
        for i in range(nocc):
            for j in range(nocc):
                value = 2.0 * amps[i, j] - amps[j, i]
                mixed_ref[i, :, pl.ds(j * narrow, narrow)] = value.astype(BF)

    vmem = pl.BlockSpec(memory_space=pltpu.VMEM)
    return pl.pallas_call(
        body,
        out_shape=(
            jax.ShapeDtypeStruct((nocc, nocc, share, narrow), BF),
            jax.ShapeDtypeStruct((nocc, share, nocc * narrow), BF),
        ),
        in_specs=[pl.BlockSpec(memory_space=pltpu.SMEM), vmem, vmem, vmem],
        out_specs=(vmem, vmem),
        compiler_params=pltpu.CompilerParams(vmem_limit_bytes=12 * 1024 * 1024),
        name="amplitudes_of",
    )(slot, row_energy, col_energy, parts)


def place(value, nocc):
    nz, r, lanes = value.shape
    narrow = lanes // nocc
    nl = nz // 2

    def body(value_ref, out_ref):
        for i in range(nocc):
            for k in range(nz):
                block = (k % nl + nl // 2) % nl * 2 + k // nl
                out_ref[i, :, pl.ds(block * narrow, narrow)] = value_ref[k, :, pl.ds(i * narrow, narrow)]

    vmem = pl.BlockSpec(memory_space=pltpu.VMEM)
    return pl.pallas_call(
        body,
        out_shape=jax.ShapeDtypeStruct((nocc, r, nz * narrow), BF),
        in_specs=[vmem],
        out_specs=vmem,
        compiler_params=pltpu.CompilerParams(vmem_limit_bytes=12 * 1024 * 1024),
        name="place",
    )(value)


def local(half_ints, coef_virt, screen, occ_energy, virt_energy, batch_orbitals):
    p_rows, nocc, ao_part = half_ints.shape
    nv = virt_energy.shape[0]
    nx, nz, ny = lax.axis_size("x"), lax.axis_size("z"), lax.axis_size("y")
    nl = nz // 2
    x, z, c, y = (lax.axis_index(name) for name in ("x", "z", "c", "y"))
    zh, zl = z // nl, z % nl
    r = p_rows // ny
    wide = nv // nx
    narrow = nv // nz
    half = wide // 2
    share = half // ny
    ways = wide // narrow

    labels = jnp.arange(occ_energy.shape[0], dtype=jnp.int32)
    onehot = (batch_orbitals[:, None] == labels[None, :]).astype(F32)
    slot_energy = jnp.sum(onehot * occ_energy[None, :], axis=1)

    with jax.named_scope("transform"):
        coef = exchange(spread(coef_virt, nz), "z")
        expanded = jnp.repeat(jnp.repeat(screen, 32, axis=0), 128, axis=1).astype(BF)
        masked = half_ints * expanded[:, None, :]
        masked = masked.reshape(ny, r, nocc, ao_part).transpose(0, 2, 1, 3)
        masked = lax.all_gather(masked.reshape(-1, ao_part), "x", axis=0)
        masked = masked.reshape(nx, ny, nocc, r, ao_part)
        masked, coef = lax.optimization_barrier((masked, coef))
        low, high = by_core(coef, swap_cores(coef), c)
        coef = jnp.stack([low, high], axis=1).reshape(wide, ao_part)
        part = jnp.einsum("xyirm,am->yxira", masked, coef, preferred_element_type=F32)
        part = exchange(part.astype(BF).reshape(ny, nx * nocc * r, wide), "y")
        three = jnp.sum(part.astype(F32), axis=0).astype(BF).reshape(nx, nocc, r, wide)

    with jax.named_scope("panels"):
        row = jnp.concatenate([three[:, i] for i in range(nocc)], axis=-1)
        row = lax.all_gather(row.reshape(nx * r, nocc * wide), "z", axis=0, tiled=True)
        col = exchange(three.reshape(nx, nocc * r, wide), "x")
        col = jnp.roll(col, nx // 2, axis=0).reshape(nx, nocc, r, ways // 2, 2, narrow)
        col = jnp.concatenate(
            [col[:, i].transpose(3, 0, 2, 1, 4).reshape(nz, r, narrow) for i in range(nocc)], axis=-1
        )
        col = exchange(col, "z")
        col = lax.all_gather(col.reshape(nz * r, nocc * narrow), "x", axis=0)
        col = col.reshape(nx, nz, r, nocc * narrow)

    with jax.named_scope("gram"):
        other = swap_cores(gram_half(row, col, 1 - c, nocc, ny, BF))
        gram = gram_half(row, col, c, nocc, ny, F32) + other.astype(F32)
        gram = exchange(gram.astype(BF).reshape(ny, nocc * share, nocc * narrow), "y")

    with jax.named_scope("amplitudes"):
        row_energy = lax.dynamic_slice_in_dim(virt_energy, x * wide + c * half + y * share, share, 0)
        col_energy = lax.dynamic_slice_in_dim(virt_energy, ((zl + nl // 2) % nl * 2 + zh) * narrow, narrow, 0)
        amps, mixed = amplitudes_of(gram, slot_energy, row_energy[:, None], col_energy[None, :])
        swap = []
        for h in range(2):
            for l in range(nl):
                for k in range(2):
                    swap.append(((h * nl + l) * 2 + k, (k * nl + (l + nl // 2) % nl) * 2 + h))
        own = lax.ppermute(amps, ("z", "c"), swap)
        mixed = lax.all_gather(mixed.reshape(nocc * share, nocc * narrow), "y", axis=0)
        mixed = mixed.reshape(ny, nocc, share, nocc * narrow)
        theirs = swap_cores(mixed)

    with jax.named_scope("gamma"):
        value = contract(row, theirs, 1 - c, nx, nz, contract(row, mixed, c, nx, nz))
        value = exchange(value.reshape(nx, nz * r, nocc * narrow), "x")
        value = jnp.sum(value.astype(F32), axis=0).astype(BF)
        value, own = lax.optimization_barrier((value, own))
        value = exchange(value.reshape(nz, r, nocc * narrow), "z")
        gamma = place(value, nocc)
    return own.astype(F32).transpose(0, 2, 1, 3)[None], gamma.transpose(1, 0, 2)


def solution(mesh):
    fine = Mesh(mesh.devices.reshape(4, mesh.shape["aux"] // 8, 2, mesh.shape["occ"]), ("x", "z", "c", "y"))
    aux = ("x", "z", "c")
    in_specs = (P(aux, None, "y"), P(aux, "y"), P(aux, "y"), P(), P(), P())
    out_specs = (P(aux, None, "y", None, None), P(aux + ("y",), None, None))
    return jax.shard_map(local, mesh=fine, in_specs=in_specs, out_specs=out_specs, check_vma=False)
```

```python
import jax
import jax.numpy as jnp
from jax import lax
from jax.experimental import pallas as pl
from jax.experimental.pallas import tpu as pltpu
from jax.sharding import Mesh
from jax.sharding import PartitionSpec as P

BF = jnp.bfloat16
F32 = jnp.float32


def swap_cores(value):
    return lax.ppermute(value, "c", [(0, 1), (1, 0)])


def exchange(value, axis):
    members, rows, lanes = value.shape
    value = value.reshape(members * rows, lanes)
    value = lax.all_to_all(value, axis, split_axis=0, concat_axis=0, tiled=True)
    return value.reshape(members, rows, lanes)


def by_core(mine, theirs, core):
    return jnp.where(core == 0, mine, theirs), jnp.where(core == 0, theirs, mine)


def spread(value, copies):
    def body(value_ref, out_ref, sems):
        moves = [pltpu.make_async_copy(value_ref, out_ref.at[k], sems.at[k]) for k in range(copies)]
        for move in moves:
            move.start()
        for move in moves:
            move.wait()

    return pl.pallas_call(
        body,
        out_shape=pltpu.HBM((copies,) + value.shape, value.dtype),
        in_specs=[pl.BlockSpec(memory_space=pl.ANY)],
        out_specs=pl.BlockSpec(memory_space=pltpu.HBM),
        scratch_shapes=[pltpu.SemaphoreType.DMA((copies,))],
        compiler_params=pltpu.CompilerParams(vmem_limit_bytes=12 * 1024 * 1024),
        name="spread",
    )(value)


def add_parts(parts, nx, nocc):
    ways, rows, wide = parts.shape
    r = rows // nx // nocc

    def body(parts_ref, row_ref, three_ref):
        total = parts_ref[0].astype(F32)
        for k in range(1, ways):
            total = total + parts_ref[k].astype(F32)
        total = total.astype(BF)
        three_ref[...] = total
        for i in range(nocc):
            row_ref[:, i * wide : (i + 1) * wide] = total[i * r : (i + 1) * r]

    return pl.pallas_call(
        body,
        out_shape=(
            pltpu.HBM((nx * r, nocc * wide), BF),
            jax.ShapeDtypeStruct((rows, wide), BF),
        ),
        grid=(nx,),
        in_specs=[pl.BlockSpec((ways, nocc * r, wide), lambda k: (0, k, 0))],
        out_specs=(
            pl.BlockSpec((r, nocc * wide), lambda k: (k, 0)),
            pl.BlockSpec((nocc * r, wide), lambda k: (k, 0)),
        ),
        compiler_params=pltpu.CompilerParams(vmem_limit_bytes=12 * 1024 * 1024),
        name="add_parts",
    )(parts)


def gram_half(row, col, which, nocc, ny, kind):
    k_rows, lanes = row.shape
    half = lanes // nocc // 2
    share = half // ny
    nx, nz, r, width = col.shape

    def body(which_ref, row_ref, col_ref, out_ref, order_ref):
        @pl.when(pl.program_id(0) == 0)
        def _():
            for k in range(nz):
                for m in range(nx):
                    order_ref[(k * nx + m) * r : (k * nx + m + 1) * r, :] = col_ref[m, k]

        tile = lax.dot_general(
            row_ref[...], order_ref[...], (((0,), (0,)), ((), ())), preferred_element_type=F32
        )
        out_ref[...] = tile.reshape(ny, 1, share, width).astype(kind)

    return pl.pallas_call(
        body,
        out_shape=jax.ShapeDtypeStruct((ny, nocc, share, width), kind),
        grid_spec=pltpu.PrefetchScalarGridSpec(
            num_scalar_prefetch=1,
            grid=(nocc,),
            in_specs=[
                pl.BlockSpec((k_rows, half), lambda i, w: (0, 2 * i + w[0])),
                pl.BlockSpec((nx, nz, r, width), lambda i, w: (0, 0, 0, 0)),
            ],
            out_specs=pl.BlockSpec((ny, 1, share, width), lambda i, w: (0, i, 0, 0)),
            scratch_shapes=[pltpu.VMEM((k_rows, width), BF)],
        ),
        compiler_params=pltpu.CompilerParams(vmem_limit_bytes=12 * 1024 * 1024),
        cost_estimate=pl.CostEstimate(
            flops=2 * k_rows * nocc * half * width,
            bytes_accessed=2 * k_rows * (nocc * half + width) + 4 * nocc * half * width,
            transcendentals=0,
        ),
        name="gram_half",
    )(which.reshape(1), row, col)


def contract(row, tile, side, nx, nz, base=None):
    k_rows, lanes = row.shape
    ny, nocc, share, width = tile.shape
    half = ny * share
    r = k_rows // nx // nz
    steps = 4
    zs = nz // steps
    size = k_rows // steps

    def body(side_ref, *refs):
        rows, tile_ref, rest = refs[:nocc], refs[nocc], refs[nocc + 1 :]
        total = jnp.zeros((size, width), F32) if base is None else rest[0][...]
        for i in range(nocc):
            total = total + jnp.dot(
                rows[i][...], tile_ref[:, i].reshape(half, width), preferred_element_type=F32
            )
        if base is None:
            rest[-1][...] = total
        else:
            value = total.astype(BF).reshape(zs, nx, r, width)
            for k in range(nx):
                rest[-1][k] = value[:, k]

    def lane_block(i):
        return pl.BlockSpec((size, half), lambda s, w: (s, 2 * i + w[0]))

    flat = pl.BlockSpec((size, width), lambda s, w: (s, 0))
    in_specs = [lane_block(i) for i in range(nocc)]
    in_specs.append(pl.BlockSpec((ny, nocc, share, width), lambda s, w: (0, 0, 0, 0)))
    if base is None:
        out_shape, out_specs, extra = jax.ShapeDtypeStruct((k_rows, width), F32), flat, ()
    else:
        in_specs.append(flat)
        out_shape = pltpu.HBM((nx, nz, r, width), BF)
        out_specs, extra = pl.BlockSpec((nx, zs, r, width), lambda s, w: (0, s, 0, 0)), (base,)
    return pl.pallas_call(
        body,
        out_shape=out_shape,
        grid_spec=pltpu.PrefetchScalarGridSpec(
            num_scalar_prefetch=1, grid=(steps,), in_specs=in_specs, out_specs=out_specs
        ),
        compiler_params=pltpu.CompilerParams(vmem_limit_bytes=12 * 1024 * 1024),
        cost_estimate=pl.CostEstimate(
            flops=k_rows * lanes * width,
            bytes_accessed=k_rows * (lanes + 4 * width) + lanes * width,
            transcendentals=0,
        ),
        name="contract",
    )(side.reshape(1), *([row] * nocc), tile, *extra)


def amplitudes_of(parts, slot, row_energy, col_energy):
    nocc = slot.shape[0]
    share, narrow = row_energy.shape[0], col_energy.shape[1]
    ways = parts.shape[0]

    def body(slot_ref, row_ref, col_ref, parts_ref, amps_ref, mixed_ref):
        amps = {}
        for i in range(nocc):
            for j in range(nocc):
                at = (pl.ds(i * share, share), pl.ds(j * narrow, narrow))
                total = parts_ref[(0,) + at].astype(F32)
                for k in range(1, ways):
                    total = total + parts_ref[(k,) + at].astype(F32)
                gap = slot_ref[i] + slot_ref[j] - row_ref[...] - col_ref[...]
                amps[i, j] = total / gap
                amps_ref[i, j] = amps[i, j].astype(BF)
        for i in range(nocc):
            for j in range(nocc):
                value = 2.0 * amps[i, j] - amps[j, i]
                mixed_ref[i, :, pl.ds(j * narrow, narrow)] = value.astype(BF)

    vmem = pl.BlockSpec(memory_space=pltpu.VMEM)
    return pl.pallas_call(
        body,
        out_shape=(
            jax.ShapeDtypeStruct((nocc, nocc, share, narrow), BF),
            jax.ShapeDtypeStruct((nocc, share, nocc * narrow), BF),
        ),
        in_specs=[pl.BlockSpec(memory_space=pltpu.SMEM), vmem, vmem, vmem],
        out_specs=(vmem, vmem),
        compiler_params=pltpu.CompilerParams(vmem_limit_bytes=12 * 1024 * 1024),
        name="amplitudes_of",
    )(slot, row_energy, col_energy, parts)


def place(value, nocc):
    nz, r, lanes = value.shape
    narrow = lanes // nocc
    nl = nz // 2

    def body(value_ref, out_ref):
        for i in range(nocc):
            for k in range(nz):
                block = (k % nl + nl // 2) % nl * 2 + k // nl
                out_ref[i, :, pl.ds(block * narrow, narrow)] = value_ref[k, :, pl.ds(i * narrow, narrow)]

    vmem = pl.BlockSpec(memory_space=pltpu.VMEM)
    return pl.pallas_call(
        body,
        out_shape=jax.ShapeDtypeStruct((nocc, r, nz * narrow), BF),
        in_specs=[vmem],
        out_specs=vmem,
        compiler_params=pltpu.CompilerParams(vmem_limit_bytes=12 * 1024 * 1024),
        name="place",
    )(value)


def local(half_ints, coef_virt, screen, occ_energy, virt_energy, batch_orbitals):
    p_rows, nocc, ao_part = half_ints.shape
    nv = virt_energy.shape[0]
    nx, nz, ny = lax.axis_size("x"), lax.axis_size("z"), lax.axis_size("y")
    nl = nz // 2
    x, z, c, y = (lax.axis_index(name) for name in ("x", "z", "c", "y"))
    zh, zl = z // nl, z % nl
    r = p_rows // ny
    wide = nv // nx
    narrow = nv // nz
    half = wide // 2
    share = half // ny
    ways = wide // narrow

    labels = jnp.arange(occ_energy.shape[0], dtype=jnp.int32)
    onehot = (batch_orbitals[:, None] == labels[None, :]).astype(F32)
    slot_energy = jnp.sum(onehot * occ_energy[None, :], axis=1)

    with jax.named_scope("transform"):
        coef = exchange(spread(coef_virt, nz), "z")
        expanded = jnp.repeat(jnp.repeat(screen, 32, axis=0), 128, axis=1).astype(BF)
        masked = half_ints * expanded[:, None, :]
        masked = masked.reshape(ny, r, nocc, ao_part).transpose(0, 2, 1, 3)
        masked = lax.all_gather(masked.reshape(-1, ao_part), "x", axis=0)
        masked = masked.reshape(nx, ny, nocc, r, ao_part)
        masked, coef = lax.optimization_barrier((masked, coef))
        low, high = by_core(coef, swap_cores(coef), c)
        coef = jnp.stack([low, high], axis=1).reshape(wide, ao_part)
        part = jnp.einsum("xyirm,am->yxira", masked, coef, preferred_element_type=F32)
        part = exchange(part.astype(BF).reshape(ny, nx * nocc * r, wide), "y")
        row, three = add_parts(part, nx, nocc)

    with jax.named_scope("panels"):
        row = lax.all_gather(row, "z", axis=0, tiled=True)
        col = exchange(three.reshape(nx, nocc * r, wide), "x")
        col = jnp.roll(col, nx // 2, axis=0).reshape(nx, nocc, r, ways // 2, 2, narrow)
        col = jnp.concatenate(
            [col[:, i].transpose(3, 0, 2, 1, 4).reshape(nz, r, narrow) for i in range(nocc)], axis=-1
        )
        col = exchange(col, "z")
        col = lax.all_gather(col.reshape(nz * r, nocc * narrow), "x", axis=0)
        col = col.reshape(nx, nz, r, nocc * narrow)

    with jax.named_scope("gram"):
        other = swap_cores(gram_half(row, col, 1 - c, nocc, ny, BF))
        gram = gram_half(row, col, c, nocc, ny, F32) + other.astype(F32)
        gram = exchange(gram.astype(BF).reshape(ny, nocc * share, nocc * narrow), "y")

    with jax.named_scope("amplitudes"):
        row_energy = lax.dynamic_slice_in_dim(virt_energy, x * wide + c * half + y * share, share, 0)
        col_energy = lax.dynamic_slice_in_dim(virt_energy, ((zl + nl // 2) % nl * 2 + zh) * narrow, narrow, 0)
        amps, mixed = amplitudes_of(gram, slot_energy, row_energy[:, None], col_energy[None, :])
        swap = []
        for h in range(2):
            for l in range(nl):
                for k in range(2):
                    swap.append(((h * nl + l) * 2 + k, (k * nl + (l + nl // 2) % nl) * 2 + h))
        own = lax.ppermute(amps, ("z", "c"), swap)
        mixed = lax.all_gather(mixed.reshape(nocc * share, nocc * narrow), "y", axis=0)
        mixed = mixed.reshape(ny, nocc, share, nocc * narrow)
        theirs = swap_cores(mixed)

    with jax.named_scope("gamma"):
        value = contract(row, theirs, 1 - c, nx, nz, contract(row, mixed, c, nx, nz))
        value = exchange(value.reshape(nx, nz * r, nocc * narrow), "x")
        value = jnp.sum(value.astype(F32), axis=0).astype(BF)
        value, own = lax.optimization_barrier((value, own))
        value = exchange(value.reshape(nz, r, nocc * narrow), "z")
        gamma = place(value, nocc)
    return own.astype(F32).transpose(0, 2, 1, 3)[None], gamma.transpose(1, 0, 2)


def solution(mesh):
    fine = Mesh(mesh.devices.reshape(4, mesh.shape["aux"] // 8, 2, mesh.shape["occ"]), ("x", "z", "c", "y"))
    aux = ("x", "z", "c")
    in_specs = (P(aux, None, "y"), P(aux, "y"), P(aux, "y"), P(), P(), P())
    out_specs = (P(aux, None, "y", None, None), P(aux + ("y",), None, None))
    return jax.shard_map(local, mesh=fine, in_specs=in_specs, out_specs=out_specs, check_vma=False)
```

```python
import jax
import jax.numpy as jnp
from jax import lax
from jax.experimental import pallas as pl
from jax.experimental.pallas import tpu as pltpu
from jax.sharding import Mesh
from jax.sharding import PartitionSpec as P

BF = jnp.bfloat16
F32 = jnp.float32


def swap_cores(value):
    return lax.ppermute(value, "c", [(0, 1), (1, 0)])


def exchange(value, axis):
    members, rows, lanes = value.shape
    value = value.reshape(members * rows, lanes)
    value = lax.all_to_all(value, axis, split_axis=0, concat_axis=0, tiled=True)
    return value.reshape(members, rows, lanes)


def by_core(mine, theirs, core):
    return jnp.where(core == 0, mine, theirs), jnp.where(core == 0, theirs, mine)


def spread(value, copies):
    def body(value_ref, out_ref, sems):
        moves = [pltpu.make_async_copy(value_ref, out_ref.at[k], sems.at[k]) for k in range(copies)]
        for move in moves:
            move.start()
        for move in moves:
            move.wait()

    return pl.pallas_call(
        body,
        out_shape=pltpu.HBM((copies,) + value.shape, value.dtype),
        in_specs=[pl.BlockSpec(memory_space=pltpu.HBM)],
        out_specs=pl.BlockSpec(memory_space=pltpu.HBM),
        scratch_shapes=[pltpu.SemaphoreType.DMA((copies,))],
        compiler_params=pltpu.CompilerParams(vmem_limit_bytes=12 * 1024 * 1024),
        name="spread",
    )(value)


def gram_half(row, col, which, nocc, ny, kind):
    k_rows, lanes = row.shape
    half = lanes // nocc // 2
    share = half // ny
    nx, nz, r, width = col.shape

    def body(which_ref, row_ref, col_ref, out_ref, order_ref):
        @pl.when(pl.program_id(0) == 0)
        def _():
            for k in range(nz):
                for m in range(nx):
                    order_ref[(k * nx + m) * r : (k * nx + m + 1) * r, :] = col_ref[m, k]

        tile = lax.dot_general(
            row_ref[...], order_ref[...], (((0,), (0,)), ((), ())), preferred_element_type=F32
        )
        out_ref[...] = tile.reshape(ny, 1, share, width).astype(kind)

    return pl.pallas_call(
        body,
        out_shape=jax.ShapeDtypeStruct((ny, nocc, share, width), kind),
        grid_spec=pltpu.PrefetchScalarGridSpec(
            num_scalar_prefetch=1,
            grid=(nocc,),
            in_specs=[
                pl.BlockSpec((k_rows, half), lambda i, w: (0, 2 * i + w[0])),
                pl.BlockSpec((nx, nz, r, width), lambda i, w: (0, 0, 0, 0)),
            ],
            out_specs=pl.BlockSpec((ny, 1, share, width), lambda i, w: (0, i, 0, 0)),
            scratch_shapes=[pltpu.VMEM((k_rows, width), BF)],
        ),
        compiler_params=pltpu.CompilerParams(vmem_limit_bytes=12 * 1024 * 1024),
        cost_estimate=pl.CostEstimate(
            flops=2 * k_rows * nocc * half * width,
            bytes_accessed=2 * k_rows * (nocc * half + width) + 4 * nocc * half * width,
            transcendentals=0,
        ),
        name="gram_half",
    )(which.reshape(1), row, col)


def contract(row, tile, side, nx, nz, base=None):
    k_rows, lanes = row.shape
    ny, nocc, share, width = tile.shape
    half = ny * share
    r = k_rows // nx // nz
    steps = 4
    zs = nz // steps
    size = k_rows // steps

    def body(side_ref, *refs):
        rows, tile_ref, rest = refs[:nocc], refs[nocc], refs[nocc + 1 :]
        total = jnp.zeros((size, width), F32) if base is None else rest[0][...]
        for i in range(nocc):
            total = total + jnp.dot(
                rows[i][...], tile_ref[:, i].reshape(half, width), preferred_element_type=F32
            )
        if base is None:
            rest[-1][...] = total
        else:
            value = total.astype(BF).reshape(zs, nx, r, width)
            for k in range(nx):
                rest[-1][k] = value[:, k]

    def lane_block(i):
        return pl.BlockSpec((size, half), lambda s, w: (s, 2 * i + w[0]))

    flat = pl.BlockSpec((size, width), lambda s, w: (s, 0))
    in_specs = [lane_block(i) for i in range(nocc)]
    in_specs.append(pl.BlockSpec((ny, nocc, share, width), lambda s, w: (0, 0, 0, 0)))
    if base is None:
        out_shape, out_specs, extra = jax.ShapeDtypeStruct((k_rows, width), F32), flat, ()
    else:
        in_specs.append(flat)
        out_shape = pltpu.HBM((nx, nz, r, width), BF)
        out_specs, extra = pl.BlockSpec((nx, zs, r, width), lambda s, w: (0, s, 0, 0)), (base,)
    return pl.pallas_call(
        body,
        out_shape=out_shape,
        grid_spec=pltpu.PrefetchScalarGridSpec(
            num_scalar_prefetch=1, grid=(steps,), in_specs=in_specs, out_specs=out_specs
        ),
        compiler_params=pltpu.CompilerParams(vmem_limit_bytes=12 * 1024 * 1024),
        cost_estimate=pl.CostEstimate(
            flops=k_rows * lanes * width,
            bytes_accessed=k_rows * (lanes + 4 * width) + lanes * width,
            transcendentals=0,
        ),
        name="contract",
    )(side.reshape(1), *([row] * nocc), tile, *extra)


def amplitudes_of(parts, slot, row_energy, col_energy):
    nocc = slot.shape[0]
    share, narrow = row_energy.shape[0], col_energy.shape[1]
    ways = parts.shape[0]

    def body(slot_ref, row_ref, col_ref, parts_ref, amps_ref, mixed_ref):
        amps = {}
        for i in range(nocc):
            for j in range(nocc):
                at = (pl.ds(i * share, share), pl.ds(j * narrow, narrow))
                total = parts_ref[(0,) + at].astype(F32)
                for k in range(1, ways):
                    total = total + parts_ref[(k,) + at].astype(F32)
                gap = slot_ref[i] + slot_ref[j] - row_ref[...] - col_ref[...]
                amps[i, j] = total / gap
                amps_ref[i, j] = amps[i, j].astype(BF)
        for i in range(nocc):
            for j in range(nocc):
                value = 2.0 * amps[i, j] - amps[j, i]
                mixed_ref[i, :, pl.ds(j * narrow, narrow)] = value.astype(BF)

    vmem = pl.BlockSpec(memory_space=pltpu.VMEM)
    return pl.pallas_call(
        body,
        out_shape=(
            jax.ShapeDtypeStruct((nocc, nocc, share, narrow), BF),
            jax.ShapeDtypeStruct((nocc, share, nocc * narrow), BF),
        ),
        in_specs=[pl.BlockSpec(memory_space=pltpu.SMEM), vmem, vmem, vmem],
        out_specs=(vmem, vmem),
        compiler_params=pltpu.CompilerParams(vmem_limit_bytes=12 * 1024 * 1024),
        name="amplitudes_of",
    )(slot, row_energy, col_energy, parts)


def place(value, nocc):
    nz, r, lanes = value.shape
    narrow = lanes // nocc
    nl = nz // 2

    def body(value_ref, out_ref):
        for i in range(nocc):
            for k in range(nz):
                block = (k % nl + nl // 2) % nl * 2 + k // nl
                out_ref[i, :, pl.ds(block * narrow, narrow)] = value_ref[k, :, pl.ds(i * narrow, narrow)]

    vmem = pl.BlockSpec(memory_space=pltpu.VMEM)
    return pl.pallas_call(
        body,
        out_shape=jax.ShapeDtypeStruct((nocc, r, nz * narrow), BF),
        in_specs=[vmem],
        out_specs=vmem,
        compiler_params=pltpu.CompilerParams(vmem_limit_bytes=12 * 1024 * 1024),
        name="place",
    )(value)


def local(half_ints, coef_virt, screen, occ_energy, virt_energy, batch_orbitals):
    p_rows, nocc, ao_part = half_ints.shape
    nv = virt_energy.shape[0]
    nx, nz, ny = lax.axis_size("x"), lax.axis_size("z"), lax.axis_size("y")
    nl = nz // 2
    x, z, c, y = (lax.axis_index(name) for name in ("x", "z", "c", "y"))
    zh, zl = z // nl, z % nl
    r = p_rows // ny
    wide = nv // nx
    narrow = nv // nz
    half = wide // 2
    share = half // ny
    ways = wide // narrow

    labels = jnp.arange(occ_energy.shape[0], dtype=jnp.int32)
    onehot = (batch_orbitals[:, None] == labels[None, :]).astype(F32)
    slot_energy = jnp.sum(onehot * occ_energy[None, :], axis=1)

    with jax.named_scope("transform"):
        coef = exchange(spread(pltpu.with_memory_space_constraint(coef_virt, pltpu.HBM), nz), "z")
        expanded = jnp.repeat(jnp.repeat(screen, 32, axis=0), 128, axis=1).astype(BF)
        masked = half_ints * expanded[:, None, :]
        masked = masked.reshape(ny, r, nocc, ao_part).transpose(0, 2, 1, 3)
        masked = lax.all_gather(masked.reshape(-1, ao_part), "x", axis=0)
        masked = masked.reshape(nx, ny, nocc, r, ao_part)
        masked, coef = lax.optimization_barrier((masked, coef))
        low, high = by_core(coef, swap_cores(coef), c)
        coef = jnp.stack([low, high], axis=1).reshape(wide, ao_part)
        part = jnp.einsum("xyirm,am->yxira", masked, coef, preferred_element_type=F32)
        part = exchange(part.astype(BF).reshape(ny, nx * nocc * r, wide), "y")
        three = jnp.sum(part.astype(F32), axis=0).astype(BF).reshape(nx, nocc, r, wide)

    with jax.named_scope("panels"):
        row = jnp.concatenate([three[:, i] for i in range(nocc)], axis=-1)
        row = lax.all_gather(row.reshape(nx * r, nocc * wide), "z", axis=0, tiled=True)
        col = exchange(three.reshape(nx, nocc * r, wide), "x")
        col = jnp.roll(col, nx // 2, axis=0).reshape(nx, nocc, r, ways // 2, 2, narrow)
        col = jnp.concatenate(
            [col[:, i].transpose(3, 0, 2, 1, 4).reshape(nz, r, narrow) for i in range(nocc)], axis=-1
        )
        col = exchange(col, "z")
        col = lax.all_gather(col.reshape(nz * r, nocc * narrow), "x", axis=0)
        col = pltpu.with_memory_space_constraint(col.reshape(nx, nz, r, nocc * narrow), pltpu.HBM)

    with jax.named_scope("gram"):
        other = swap_cores(gram_half(row, col, 1 - c, nocc, ny, BF))
        gram = gram_half(row, col, c, nocc, ny, F32) + other.astype(F32)
        gram = exchange(gram.astype(BF).reshape(ny, nocc * share, nocc * narrow), "y")

    with jax.named_scope("amplitudes"):
        row_energy = lax.dynamic_slice_in_dim(virt_energy, x * wide + c * half + y * share, share, 0)
        col_energy = lax.dynamic_slice_in_dim(virt_energy, ((zl + nl // 2) % nl * 2 + zh) * narrow, narrow, 0)
        amps, mixed = amplitudes_of(gram, slot_energy, row_energy[:, None], col_energy[None, :])
        swap = []
        for h in range(2):
            for l in range(nl):
                for k in range(2):
                    swap.append(((h * nl + l) * 2 + k, (k * nl + (l + nl // 2) % nl) * 2 + h))
        own = lax.ppermute(amps, ("z", "c"), swap)
        mixed = lax.all_gather(mixed.reshape(nocc * share, nocc * narrow), "y", axis=0)
        mixed = mixed.reshape(ny, nocc, share, nocc * narrow)
        theirs = swap_cores(mixed)

    with jax.named_scope("gamma"):
        value = contract(row, theirs, 1 - c, nx, nz, contract(row, mixed, c, nx, nz))
        value = exchange(value.reshape(nx, nz * r, nocc * narrow), "x")
        value = jnp.sum(value.astype(F32), axis=0).astype(BF)
        value, own = lax.optimization_barrier((value, own))
        value = exchange(value.reshape(nz, r, nocc * narrow), "z")
        gamma = place(value, nocc)
    return own.astype(F32).transpose(0, 2, 1, 3)[None], gamma.transpose(1, 0, 2)


def solution(mesh):
    fine = Mesh(mesh.devices.reshape(4, mesh.shape["aux"] // 8, 2, mesh.shape["occ"]), ("x", "z", "c", "y"))
    aux = ("x", "z", "c")
    in_specs = (P(aux, None, "y"), P(aux, "y"), P(aux, "y"), P(), P(), P())
    out_specs = (P(aux, None, "y", None, None), P(aux + ("y",), None, None))
    return jax.shard_map(local, mesh=fine, in_specs=in_specs, out_specs=out_specs, check_vma=False)
```

```python
import jax
import jax.numpy as jnp
from jax import lax
from jax.experimental import pallas as pl
from jax.experimental.pallas import tpu as pltpu
from jax.sharding import Mesh
from jax.sharding import PartitionSpec as P

BF = jnp.bfloat16
F32 = jnp.float32


def swap_cores(value):
    return lax.ppermute(value, "c", [(0, 1), (1, 0)])


def exchange(value, axis):
    members, rows, lanes = value.shape
    value = value.reshape(members * rows, lanes)
    value = lax.all_to_all(value, axis, split_axis=0, concat_axis=0, tiled=True)
    return value.reshape(members, rows, lanes)


def by_core(mine, theirs, core):
    return jnp.where(core == 0, mine, theirs), jnp.where(core == 0, theirs, mine)


def spread(value, copies):
    def body(value_ref, out_ref, sems):
        moves = [pltpu.make_async_copy(value_ref, out_ref.at[k], sems.at[k]) for k in range(copies)]
        for move in moves:
            move.start()
        for move in moves:
            move.wait()

    return pl.pallas_call(
        body,
        out_shape=pltpu.HBM((copies,) + value.shape, value.dtype),
        in_specs=[pl.BlockSpec(memory_space=pltpu.VMEM)],
        out_specs=pl.BlockSpec(memory_space=pltpu.HBM),
        scratch_shapes=[pltpu.SemaphoreType.DMA((copies,))],
        compiler_params=pltpu.CompilerParams(vmem_limit_bytes=12 * 1024 * 1024),
        name="spread",
    )(value)


def gram_half(row, col, which, nocc, ny, kind):
    k_rows, lanes = row.shape
    half = lanes // nocc // 2
    share = half // ny
    nx, nz, r, width = col.shape

    def body(which_ref, row_ref, col_ref, out_ref, order_ref):
        @pl.when(pl.program_id(0) == 0)
        def _():
            for k in range(nz):
                for m in range(nx):
                    order_ref[(k * nx + m) * r : (k * nx + m + 1) * r, :] = col_ref[m, k]

        tile = lax.dot_general(
            row_ref[...], order_ref[...], (((0,), (0,)), ((), ())), preferred_element_type=F32
        )
        out_ref[...] = tile.reshape(ny, 1, share, width).astype(kind)

    return pl.pallas_call(
        body,
        out_shape=jax.ShapeDtypeStruct((ny, nocc, share, width), kind),
        grid_spec=pltpu.PrefetchScalarGridSpec(
            num_scalar_prefetch=1,
            grid=(nocc,),
            in_specs=[
                pl.BlockSpec((k_rows, half), lambda i, w: (0, 2 * i + w[0])),
                pl.BlockSpec((nx, nz, r, width), lambda i, w: (0, 0, 0, 0)),
            ],
            out_specs=pl.BlockSpec((ny, 1, share, width), lambda i, w: (0, i, 0, 0)),
            scratch_shapes=[pltpu.VMEM((k_rows, width), BF)],
        ),
        compiler_params=pltpu.CompilerParams(vmem_limit_bytes=12 * 1024 * 1024),
        cost_estimate=pl.CostEstimate(
            flops=2 * k_rows * nocc * half * width,
            bytes_accessed=2 * k_rows * (nocc * half + width) + 4 * nocc * half * width,
            transcendentals=0,
        ),
        name="gram_half",
    )(which.reshape(1), row, col)


def contract(row, tile, side, nx, nz, base=None):
    k_rows, lanes = row.shape
    ny, nocc, share, width = tile.shape
    half = ny * share
    r = k_rows // nx // nz
    steps = 4
    zs = nz // steps
    size = k_rows // steps

    def body(side_ref, *refs):
        rows, tile_ref, rest = refs[:nocc], refs[nocc], refs[nocc + 1 :]
        total = jnp.zeros((size, width), F32) if base is None else rest[0][...]
        for i in range(nocc):
            total = total + jnp.dot(
                rows[i][...], tile_ref[:, i].reshape(half, width), preferred_element_type=F32
            )
        if base is None:
            rest[-1][...] = total
        else:
            value = total.astype(BF).reshape(zs, nx, r, width)
            for k in range(nx):
                rest[-1][k] = value[:, k]

    def lane_block(i):
        return pl.BlockSpec((size, half), lambda s, w: (s, 2 * i + w[0]))

    flat = pl.BlockSpec((size, width), lambda s, w: (s, 0))
    in_specs = [lane_block(i) for i in range(nocc)]
    in_specs.append(pl.BlockSpec((ny, nocc, share, width), lambda s, w: (0, 0, 0, 0)))
    if base is None:
        out_shape, out_specs, extra = jax.ShapeDtypeStruct((k_rows, width), F32), flat, ()
    else:
        in_specs.append(flat)
        out_shape = pltpu.HBM((nx, nz, r, width), BF)
        out_specs, extra = pl.BlockSpec((nx, zs, r, width), lambda s, w: (0, s, 0, 0)), (base,)
    return pl.pallas_call(
        body,
        out_shape=out_shape,
        grid_spec=pltpu.PrefetchScalarGridSpec(
            num_scalar_prefetch=1, grid=(steps,), in_specs=in_specs, out_specs=out_specs
        ),
        compiler_params=pltpu.CompilerParams(vmem_limit_bytes=12 * 1024 * 1024),
        cost_estimate=pl.CostEstimate(
            flops=k_rows * lanes * width,
            bytes_accessed=k_rows * (lanes + 4 * width) + lanes * width,
            transcendentals=0,
        ),
        name="contract",
    )(side.reshape(1), *([row] * nocc), tile, *extra)


def amplitudes_of(parts, slot, row_energy, col_energy):
    nocc = slot.shape[0]
    share, narrow = row_energy.shape[0], col_energy.shape[1]
    ways = parts.shape[0]

    def body(slot_ref, row_ref, col_ref, parts_ref, amps_ref, mixed_ref):
        amps = {}
        for i in range(nocc):
            for j in range(nocc):
                at = (pl.ds(i * share, share), pl.ds(j * narrow, narrow))
                total = parts_ref[(0,) + at].astype(F32)
                for k in range(1, ways):
                    total = total + parts_ref[(k,) + at].astype(F32)
                gap = slot_ref[i] + slot_ref[j] - row_ref[...] - col_ref[...]
                amps[i, j] = total / gap
                amps_ref[i, j] = amps[i, j].astype(BF)
        for i in range(nocc):
            for j in range(nocc):
                value = 2.0 * amps[i, j] - amps[j, i]
                mixed_ref[i, :, pl.ds(j * narrow, narrow)] = value.astype(BF)

    vmem = pl.BlockSpec(memory_space=pltpu.VMEM)
    return pl.pallas_call(
        body,
        out_shape=(
            jax.ShapeDtypeStruct((nocc, nocc, share, narrow), BF),
            jax.ShapeDtypeStruct((nocc, share, nocc * narrow), BF),
        ),
        in_specs=[pl.BlockSpec(memory_space=pltpu.SMEM), vmem, vmem, vmem],
        out_specs=(vmem, vmem),
        compiler_params=pltpu.CompilerParams(vmem_limit_bytes=12 * 1024 * 1024),
        name="amplitudes_of",
    )(slot, row_energy, col_energy, parts)


def place(value, nocc):
    nz, r, lanes = value.shape
    narrow = lanes // nocc
    nl = nz // 2

    def body(value_ref, out_ref):
        for i in range(nocc):
            for k in range(nz):
                block = (k % nl + nl // 2) % nl * 2 + k // nl
                out_ref[i, :, pl.ds(block * narrow, narrow)] = value_ref[k, :, pl.ds(i * narrow, narrow)]

    vmem = pl.BlockSpec(memory_space=pltpu.VMEM)
    return pl.pallas_call(
        body,
        out_shape=jax.ShapeDtypeStruct((nocc, r, nz * narrow), BF),
        in_specs=[vmem],
        out_specs=vmem,
        compiler_params=pltpu.CompilerParams(vmem_limit_bytes=12 * 1024 * 1024),
        name="place",
    )(value)


def local(half_ints, coef_virt, screen, occ_energy, virt_energy, batch_orbitals):
    p_rows, nocc, ao_part = half_ints.shape
    nv = virt_energy.shape[0]
    nx, nz, ny = lax.axis_size("x"), lax.axis_size("z"), lax.axis_size("y")
    nl = nz // 2
    x, z, c, y = (lax.axis_index(name) for name in ("x", "z", "c", "y"))
    zh, zl = z // nl, z % nl
    r = p_rows // ny
    wide = nv // nx
    narrow = nv // nz
    half = wide // 2
    share = half // ny
    ways = wide // narrow

    labels = jnp.arange(occ_energy.shape[0], dtype=jnp.int32)
    onehot = (batch_orbitals[:, None] == labels[None, :]).astype(F32)
    slot_energy = jnp.sum(onehot * occ_energy[None, :], axis=1)

    with jax.named_scope("transform"):
        coef = exchange(spread(coef_virt, nz), "z")
        expanded = jnp.repeat(jnp.repeat(screen, 32, axis=0), 128, axis=1).astype(BF)
        masked = half_ints * expanded[:, None, :]
        masked = masked.reshape(ny, r, nocc, ao_part).transpose(0, 2, 1, 3)
        masked = lax.all_gather(masked.reshape(-1, ao_part), "x", axis=0)
        masked = masked.reshape(nx, ny, nocc, r, ao_part)
        masked, coef = lax.optimization_barrier((masked, coef))
        low, high = by_core(coef, swap_cores(coef), c)
        coef = jnp.stack([low, high], axis=1).reshape(wide, ao_part)
        part = jnp.einsum("xyirm,am->yxira", masked, coef, preferred_element_type=F32)
        part = exchange(part.astype(BF).reshape(ny, nx * nocc * r, wide), "y")
        three = jnp.sum(part.astype(F32), axis=0).astype(BF).reshape(nx, nocc, r, wide)

    with jax.named_scope("panels"):
        row = jnp.concatenate([three[:, i] for i in range(nocc)], axis=-1)
        row = lax.all_gather(row.reshape(nx * r, nocc * wide), "z", axis=0, tiled=True)
        col = exchange(three.reshape(nx, nocc * r, wide), "x")
        col = jnp.roll(col, nx // 2, axis=0).reshape(nx, nocc, r, ways // 2, 2, narrow)
        col = jnp.concatenate(
            [col[:, i].transpose(3, 0, 2, 1, 4).reshape(nz, r, narrow) for i in range(nocc)], axis=-1
        )
        col = exchange(col, "z")
        col = lax.all_gather(col.reshape(nz * r, nocc * narrow), "x", axis=0)
        col = col.reshape(nx, nz, r, nocc * narrow)
        row_energy = lax.dynamic_slice_in_dim(virt_energy, x * wide + c * half + y * share, share, 0)
        col_energy = lax.dynamic_slice_in_dim(virt_energy, ((zl + nl // 2) % nl * 2 + zh) * narrow, narrow, 0)
        row_energy = jnp.broadcast_to(row_energy[:, None], (share, narrow))
        col_energy = col_energy[None, :]
        col, slot_energy, row_energy, col_energy = lax.optimization_barrier(
            (col, slot_energy, row_energy, col_energy)
        )

    with jax.named_scope("gram"):
        other = swap_cores(gram_half(row, col, 1 - c, nocc, ny, BF))
        gram = gram_half(row, col, c, nocc, ny, F32) + other.astype(F32)
        gram = exchange(gram.astype(BF).reshape(ny, nocc * share, nocc * narrow), "y")

    with jax.named_scope("amplitudes"):
        amps, mixed = amplitudes_of(gram, slot_energy, row_energy, col_energy)
        swap = []
        for h in range(2):
            for l in range(nl):
                for k in range(2):
                    swap.append(((h * nl + l) * 2 + k, (k * nl + (l + nl // 2) % nl) * 2 + h))
        own = lax.ppermute(amps, ("z", "c"), swap)
        mixed = lax.all_gather(mixed.reshape(nocc * share, nocc * narrow), "y", axis=0)
        mixed = mixed.reshape(ny, nocc, share, nocc * narrow)
        theirs = swap_cores(mixed)

    with jax.named_scope("gamma"):
        value = contract(row, theirs, 1 - c, nx, nz, contract(row, mixed, c, nx, nz))
        value = exchange(value.reshape(nx, nz * r, nocc * narrow), "x")
        value = jnp.sum(value.astype(F32), axis=0).astype(BF)
        value, own = lax.optimization_barrier((value, own))
        value = exchange(value.reshape(nz, r, nocc * narrow), "z")
        gamma = place(value, nocc)
    return own.astype(F32).transpose(0, 2, 1, 3)[None], gamma.transpose(1, 0, 2)


def solution(mesh):
    fine = Mesh(mesh.devices.reshape(4, mesh.shape["aux"] // 8, 2, mesh.shape["occ"]), ("x", "z", "c", "y"))
    aux = ("x", "z", "c")
    in_specs = (P(aux, None, "y"), P(aux, "y"), P(aux, "y"), P(), P(), P())
    out_specs = (P(aux, None, "y", None, None), P(aux + ("y",), None, None))
    return jax.shard_map(local, mesh=fine, in_specs=in_specs, out_specs=out_specs, check_vma=False)
```

```python
import jax
import jax.numpy as jnp
from jax import lax
from jax.experimental import pallas as pl
from jax.experimental.pallas import tpu as pltpu
from jax.sharding import Mesh
from jax.sharding import PartitionSpec as P

BF = jnp.bfloat16
F32 = jnp.float32


def swap_cores(value):
    return lax.ppermute(value, "c", [(0, 1), (1, 0)])


def exchange(value, axis):
    members, rows, lanes = value.shape
    value = value.reshape(members * rows, lanes)
    value = lax.all_to_all(value, axis, split_axis=0, concat_axis=0, tiled=True)
    return value.reshape(members, rows, lanes)


def by_core(mine, theirs, core):
    return jnp.where(core == 0, mine, theirs), jnp.where(core == 0, theirs, mine)


def spread(value, copies):
    def body(value_ref, out_ref, sems):
        moves = [pltpu.make_async_copy(value_ref, out_ref.at[k], sems.at[k]) for k in range(copies)]
        for move in moves:
            move.start()
        for move in moves:
            move.wait()

    return pl.pallas_call(
        body,
        out_shape=pltpu.HBM((copies,) + value.shape, value.dtype),
        in_specs=[pl.BlockSpec(memory_space=pltpu.VMEM)],
        out_specs=pl.BlockSpec(memory_space=pltpu.HBM),
        scratch_shapes=[pltpu.SemaphoreType.DMA((copies,))],
        compiler_params=pltpu.CompilerParams(vmem_limit_bytes=12 * 1024 * 1024),
        name="spread",
    )(value)


def gram_half(row, col, which, nocc, ny, kind):
    k_rows, lanes = row.shape
    half = lanes // nocc // 2
    share = half // ny
    nx, nz, r, width = col.shape

    def body(which_ref, row_ref, col_ref, out_ref, order_ref):
        @pl.when(pl.program_id(0) == 0)
        def _():
            for k in range(nz):
                for m in range(nx):
                    order_ref[(k * nx + m) * r : (k * nx + m + 1) * r, :] = col_ref[m, k]

        tile = lax.dot_general(
            row_ref[...], order_ref[...], (((0,), (0,)), ((), ())), preferred_element_type=F32
        )
        out_ref[...] = tile.reshape(ny, 1, share, width).astype(kind)

    return pl.pallas_call(
        body,
        out_shape=jax.ShapeDtypeStruct((ny, nocc, share, width), kind),
        grid_spec=pltpu.PrefetchScalarGridSpec(
            num_scalar_prefetch=1,
            grid=(nocc,),
            in_specs=[
                pl.BlockSpec((k_rows, half), lambda i, w: (0, 2 * i + w[0])),
                pl.BlockSpec((nx, nz, r, width), lambda i, w: (0, 0, 0, 0)),
            ],
            out_specs=pl.BlockSpec((ny, 1, share, width), lambda i, w: (0, i, 0, 0)),
            scratch_shapes=[pltpu.VMEM((k_rows, width), BF)],
        ),
        compiler_params=pltpu.CompilerParams(vmem_limit_bytes=12 * 1024 * 1024),
        cost_estimate=pl.CostEstimate(
            flops=2 * k_rows * nocc * half * width,
            bytes_accessed=2 * k_rows * (nocc * half + width) + 4 * nocc * half * width,
            transcendentals=0,
        ),
        name="gram_half",
    )(which.reshape(1), row, col)


def contract(row, tile, side, nx, nz, base=None):
    k_rows, lanes = row.shape
    ny, nocc, share, width = tile.shape
    half = ny * share
    r = k_rows // nx // nz
    steps = 4
    zs = nz // steps
    size = k_rows // steps

    def body(side_ref, *refs):
        rows, tile_ref, rest = refs[:nocc], refs[nocc], refs[nocc + 1 :]
        total = jnp.zeros((size, width), F32) if base is None else rest[0][...]
        for i in range(nocc):
            total = total + jnp.dot(
                rows[i][...], tile_ref[:, i].reshape(half, width), preferred_element_type=F32
            )
        if base is None:
            rest[-1][...] = total
        else:
            value = total.astype(BF).reshape(zs, nx, r, width)
            for k in range(nx):
                rest[-1][k] = value[:, k]

    def lane_block(i):
        return pl.BlockSpec((size, half), lambda s, w: (s, 2 * i + w[0]))

    flat = pl.BlockSpec((size, width), lambda s, w: (s, 0))
    in_specs = [lane_block(i) for i in range(nocc)]
    in_specs.append(pl.BlockSpec((ny, nocc, share, width), lambda s, w: (0, 0, 0, 0)))
    if base is None:
        out_shape, out_specs, extra = jax.ShapeDtypeStruct((k_rows, width), F32), flat, ()
    else:
        in_specs.append(flat)
        out_shape = jax.ShapeDtypeStruct((nx, nz, r, width), BF)
        out_specs, extra = pl.BlockSpec((nx, zs, r, width), lambda s, w: (0, s, 0, 0)), (base,)
    return pl.pallas_call(
        body,
        out_shape=out_shape,
        grid_spec=pltpu.PrefetchScalarGridSpec(
            num_scalar_prefetch=1, grid=(steps,), in_specs=in_specs, out_specs=out_specs
        ),
        compiler_params=pltpu.CompilerParams(vmem_limit_bytes=12 * 1024 * 1024),
        cost_estimate=pl.CostEstimate(
            flops=k_rows * lanes * width,
            bytes_accessed=k_rows * (lanes + 4 * width) + lanes * width,
            transcendentals=0,
        ),
        name="contract",
    )(side.reshape(1), *([row] * nocc), tile, *extra)


def amplitudes_of(parts, slot, row_energy, col_energy):
    nocc = slot.shape[0]
    share, narrow = row_energy.shape[0], col_energy.shape[1]
    ways = parts.shape[0]

    def body(slot_ref, row_ref, col_ref, parts_ref, amps_ref, mixed_ref):
        amps = {}
        for i in range(nocc):
            for j in range(nocc):
                at = (pl.ds(i * share, share), pl.ds(j * narrow, narrow))
                total = parts_ref[(0,) + at].astype(F32)
                for k in range(1, ways):
                    total = total + parts_ref[(k,) + at].astype(F32)
                gap = slot_ref[i] + slot_ref[j] - row_ref[...] - col_ref[...]
                amps[i, j] = total / gap
                amps_ref[i, j] = amps[i, j].astype(BF)
        for i in range(nocc):
            for j in range(nocc):
                value = 2.0 * amps[i, j] - amps[j, i]
                mixed_ref[i, :, pl.ds(j * narrow, narrow)] = value.astype(BF)

    vmem = pl.BlockSpec(memory_space=pltpu.VMEM)
    return pl.pallas_call(
        body,
        out_shape=(
            jax.ShapeDtypeStruct((nocc, nocc, share, narrow), BF),
            jax.ShapeDtypeStruct((nocc, share, nocc * narrow), BF),
        ),
        in_specs=[pl.BlockSpec(memory_space=pltpu.SMEM), vmem, vmem, vmem],
        out_specs=(vmem, vmem),
        compiler_params=pltpu.CompilerParams(vmem_limit_bytes=12 * 1024 * 1024),
        name="amplitudes_of",
    )(slot, row_energy, col_energy, parts)


def place(value, nocc):
    nz, r, lanes = value.shape
    narrow = lanes // nocc
    nl = nz // 2

    def body(value_ref, out_ref):
        for i in range(nocc):
            for k in range(nz):
                block = (k % nl + nl // 2) % nl * 2 + k // nl
                out_ref[i, :, pl.ds(block * narrow, narrow)] = value_ref[k, :, pl.ds(i * narrow, narrow)]

    vmem = pl.BlockSpec(memory_space=pltpu.VMEM)
    return pl.pallas_call(
        body,
        out_shape=jax.ShapeDtypeStruct((nocc, r, nz * narrow), BF),
        in_specs=[vmem],
        out_specs=vmem,
        compiler_params=pltpu.CompilerParams(vmem_limit_bytes=12 * 1024 * 1024),
        name="place",
    )(value)


def local(half_ints, coef_virt, screen, occ_energy, virt_energy, batch_orbitals):
    p_rows, nocc, ao_part = half_ints.shape
    nv = virt_energy.shape[0]
    nx, nz, ny = lax.axis_size("x"), lax.axis_size("z"), lax.axis_size("y")
    nl = nz // 2
    x, z, c, y = (lax.axis_index(name) for name in ("x", "z", "c", "y"))
    zh, zl = z // nl, z % nl
    r = p_rows // ny
    wide = nv // nx
    narrow = nv // nz
    half = wide // 2
    share = half // ny
    ways = wide // narrow

    labels = jnp.arange(occ_energy.shape[0], dtype=jnp.int32)
    onehot = (batch_orbitals[:, None] == labels[None, :]).astype(F32)
    slot_energy = jnp.sum(onehot * occ_energy[None, :], axis=1)

    with jax.named_scope("transform"):
        coef = exchange(spread(coef_virt, nz), "z")
        expanded = jnp.repeat(jnp.repeat(screen, 32, axis=0), 128, axis=1).astype(BF)
        masked = half_ints * expanded[:, None, :]
        masked = masked.reshape(ny, r, nocc, ao_part).transpose(0, 2, 1, 3)
        masked = lax.all_gather(masked.reshape(-1, ao_part), "x", axis=0)
        masked = masked.reshape(nx, ny, nocc, r, ao_part)
        masked, coef = lax.optimization_barrier((masked, coef))
        low, high = by_core(coef, swap_cores(coef), c)
        coef = jnp.stack([low, high], axis=1).reshape(wide, ao_part)
        part = jnp.einsum("xyirm,am->yxira", masked, coef, preferred_element_type=F32)
        part = exchange(part.astype(BF).reshape(ny, nx * nocc * r, wide), "y")
        three = jnp.sum(part.astype(F32), axis=0).astype(BF).reshape(nx, nocc, r, wide)

    with jax.named_scope("panels"):
        row = jnp.concatenate([three[:, i] for i in range(nocc)], axis=-1)
        row = lax.all_gather(row.reshape(nx * r, nocc * wide), "z", axis=0, tiled=True)
        col = exchange(three.reshape(nx, nocc * r, wide), "x")
        col = jnp.roll(col, nx // 2, axis=0).reshape(nx, nocc, r, ways // 2, 2, narrow)
        col = jnp.concatenate(
            [col[:, i].transpose(3, 0, 2, 1, 4).reshape(nz, r, narrow) for i in range(nocc)], axis=-1
        )
        col = exchange(col, "z")
        col = lax.all_gather(col.reshape(nz * r, nocc * narrow), "x", axis=0)
        col = col.reshape(nx, nz, r, nocc * narrow)
        row_energy = lax.dynamic_slice_in_dim(virt_energy, x * wide + c * half + y * share, share, 0)
        col_energy = lax.dynamic_slice_in_dim(virt_energy, ((zl + nl // 2) % nl * 2 + zh) * narrow, narrow, 0)
        row_energy = jnp.broadcast_to(row_energy[:, None], (share, narrow))
        col_energy = col_energy[None, :]
        col, slot_energy, row_energy, col_energy = lax.optimization_barrier(
            (col, slot_energy, row_energy, col_energy)
        )

    with jax.named_scope("gram"):
        other = swap_cores(gram_half(row, col, 1 - c, nocc, ny, BF))
        gram = gram_half(row, col, c, nocc, ny, F32) + other.astype(F32)
        gram = exchange(gram.astype(BF).reshape(ny, nocc * share, nocc * narrow), "y")

    with jax.named_scope("amplitudes"):
        amps, mixed = amplitudes_of(gram, slot_energy, row_energy, col_energy)
        swap = []
        for h in range(2):
            for l in range(nl):
                for k in range(2):
                    swap.append(((h * nl + l) * 2 + k, (k * nl + (l + nl // 2) % nl) * 2 + h))
        own = lax.ppermute(amps, ("z", "c"), swap)
        mixed = lax.all_gather(mixed.reshape(nocc * share, nocc * narrow), "y", axis=0)
        mixed = mixed.reshape(ny, nocc, share, nocc * narrow)
        theirs = swap_cores(mixed)

    with jax.named_scope("gamma"):
        value = contract(row, theirs, 1 - c, nx, nz, contract(row, mixed, c, nx, nz))
        value = exchange(value.reshape(nx, nz * r, nocc * narrow), "x")
        value = jnp.sum(value.astype(F32), axis=0).astype(BF)
        value = exchange(value.reshape(nz, r, nocc * narrow), "z")
        gamma = place(value, nocc)
    return own.astype(F32).transpose(0, 2, 1, 3)[None], gamma.transpose(1, 0, 2)


def solution(mesh):
    fine = Mesh(mesh.devices.reshape(4, mesh.shape["aux"] // 8, 2, mesh.shape["occ"]), ("x", "z", "c", "y"))
    aux = ("x", "z", "c")
    in_specs = (P(aux, None, "y"), P(aux, "y"), P(aux, "y"), P(), P(), P())
    out_specs = (P(aux, None, "y", None, None), P(aux + ("y",), None, None))
    return jax.shard_map(local, mesh=fine, in_specs=in_specs, out_specs=out_specs, check_vma=False)
```
